512 devices in a mesh: wide: 64 (over y, z), narrow: 8 (over x, core).
Axes of the slice: x: 4, y: 8, z: 8, core: 2. Of those that a mesh axis runs over, the one named last changes fastest.
Arguments:
- amplitudes: bfloat16 [1024, 1024, 128], P('wide', 'narrow'), may hold values from -6 to 6
- send_list: int32 [64, 128], P('wide'), may hold values from 0 to 15
- tile_positions: int32 [512, 16], P('wide', 'narrow'), may hold values from 0 to 127
- integrals: bfloat16 [512, 16, 128, 128], P('wide', 'narrow'), may hold values from -0.125 to 0.125
Outputs:
- ladder: bfloat16 [512, 1024, 128], P('wide', 'narrow')
The draws below stay inside these ranges and needn't reach their ends.
All inputs are finite; a program needn't handle non-finite values.
Results may differ from the reference program's by a relative error of at most 0.001.
Values may be sent and summed in bfloat16 or wider, within the bound.
A program may use at most 64 MiB of HBM per device.

```python
import jax
import jax.numpy as jnp
from jax import lax

TILE = 128
XT_DEV = 8
AMP_DEV = 16
KI = 16
CAP = 2
PAIRS = 1024
NX = 512
NY = 1024
N_WIDE = 64


def touch_ends(drawn, own_key, smallest, top_value):
    longest = drawn.shape.index(max(drawn.shape))
    spots = []
    for shift in (0, 1):
        where = [jax.random.randint(jax.random.fold_in(own_key, axis), (), 0, length) for axis, length in enumerate(drawn.shape)]
        where[longest] = (where[longest] + shift) % drawn.shape[longest]
        spots.append(tuple(where))
    return drawn.at[spots[0]].set(smallest).at[spots[1]].set(top_value)


def level_of(key, dims, cuts, smallest, top_value):
    level = 1.0
    for dim, blocks in cuts:
        draws = jax.random.uniform(jax.random.fold_in(jax.random.fold_in(key, 6), dim), (blocks,), jnp.float32, smallest / len(cuts), top_value / len(cuts))
        level = level * jnp.repeat(jnp.exp(draws), dims[dim] // blocks).reshape((-1,) + (1,) * (len(dims) - 1 - dim))
    return level


def bell_draw(key, dims, deviation, reach, pieces=(), kind=jnp.bfloat16):
    values = deviation * jax.random.normal(key, dims, jnp.float32)
    if pieces:
        values = values * level_of(key, dims, pieces, -0.22, 0.18)
    return jnp.clip(values, -reach, reach).astype(kind)


def setup_inputs(seed: int = 0) -> dict:
    keys = jax.random.split(jax.random.key(seed), 5)
    amplitudes = bell_draw(keys[0], (NY, PAIRS, TILE), 1.0, 6.0, ((0, 64), (1, 8)))
    send_list = touch_ends(jax.random.randint(keys[1], (N_WIDE, N_WIDE * CAP), 0, AMP_DEV), jax.random.fold_in(keys[1], 1), 0, AMP_DEV - 1).astype(jnp.int32)
    tile_positions = touch_ends(jax.random.randint(keys[2], (NX, KI), 0, N_WIDE * CAP), jax.random.fold_in(keys[2], 1), 0, (N_WIDE * CAP) - 1).astype(jnp.int32)
    integrals = bell_draw(keys[3], (NX, KI, TILE, TILE), (KI * TILE) ** -0.5, 0.125, ((0, 64), (1, 8)))
    return dict(amplitudes=amplitudes, send_list=send_list, tile_positions=tile_positions, integrals=integrals)


def reference(amplitudes, send_list, tile_positions, integrals):
    rows = jnp.arange(NX, dtype=jnp.int32)[:, None]
    device = rows // XT_DEV
    owner = tile_positions // CAP
    slot = tile_positions % CAP
    source = owner * AMP_DEV + send_list[owner, device * CAP + slot]

    def one_tile(args):
        picks, blocks = args
        tiles = amplitudes[picks]
        flat = jnp.transpose(tiles, (1, 0, 2)).reshape(PAIRS, KI * TILE)
        return jnp.dot(flat, blocks.reshape(KI * TILE, TILE), preferred_element_type=jnp.float32).astype(jnp.bfloat16)

    return lax.map(one_tile, (source.astype(jnp.int32), integrals))
```

```python
import functools

import jax
import jax.numpy as jnp
from jax import lax
from jax.experimental import pallas as pl
from jax.experimental.pallas import tpu as pltpu
from jax.sharding import PartitionSpec as P

MESH = pl.DeviceIdType.MESH


def exchange_kernel(n_wide, cap, out_hbm, recv_hbm, send_sem, recv_sem, local_sem):
    me = lax.axis_index("wide")
    nar = lax.axis_index("narrow")

    barrier = pltpu.get_barrier_semaphore()

    def greet(i, c):
        peer = lax.rem(me + i, n_wide)
        pl.semaphore_signal(barrier, 1, device_id=(peer, nar), device_id_type=MESH)
        return c

    lax.fori_loop(1, n_wide, greet, 0)
    pl.semaphore_wait(barrier, n_wide - 1)

    def block(ref, j):
        return ref.at[pl.ds(pl.multiple_of(j * cap, cap), cap)]

    local = pltpu.make_async_copy(block(out_hbm, me), block(recv_hbm, me), local_sem)
    local.start()

    def remote(peer, src_owner):
        return pltpu.make_async_remote_copy(
            src_ref=block(out_hbm, peer),
            dst_ref=block(recv_hbm, src_owner),
            send_sem=send_sem.at[peer],
            recv_sem=recv_sem.at[src_owner],
            device_id=(peer, nar),
            device_id_type=MESH,
        )

    def send(i, c):
        peer = lax.rem(me + i, n_wide)
        remote(peer, me).start()
        return c

    lax.fori_loop(1, n_wide, send, 0)

    def finish(i, c):
        peer = lax.rem(me + i, n_wide)
        remote(peer, me).wait_send()
        owner = lax.rem(me + n_wide - i, n_wide)
        remote(owner, owner).wait_recv()
        return c

    lax.fori_loop(1, n_wide, finish, 0)
    local.wait()


def exchange(outgoing, n_wide, cap):
    return pl.pallas_call(
        functools.partial(exchange_kernel, n_wide, cap),
        out_shape=jax.ShapeDtypeStruct(outgoing.shape, outgoing.dtype),
        in_specs=[pl.BlockSpec(memory_space=pl.ANY)],
        out_specs=pl.BlockSpec(memory_space=pl.ANY),
        scratch_shapes=[
            pltpu.SemaphoreType.DMA((n_wide,)),
            pltpu.SemaphoreType.DMA((n_wide,)),
            pltpu.SemaphoreType.DMA,
        ],
        compiler_params=pltpu.CompilerParams(collective_id=0, has_side_effects=True),
    )(outgoing)


def on_device(n_wide, amplitudes, send_list, tile_positions, integrals):
    cap = send_list.shape[1] // n_wide
    outgoing = amplitudes[send_list[0]]
    received = exchange(outgoing, n_wide, cap)
    start_sum = jnp.zeros((integrals.shape[0], received.shape[1], integrals.shape[3]), jnp.float32)
    blocks = lax.all_gather(integrals, "narrow", axis=1, tiled=True)
    places = lax.all_gather(tile_positions, "narrow", axis=1, tiled=True)
    picked = received[places]
    total = start_sum + jnp.einsum(
        "xmpt,xmts->xps", picked, blocks, preferred_element_type=jnp.float32
    )
    return total.astype(jnp.bfloat16)


def solution(mesh):
    placed = (
        P("wide", "narrow", None),
        P("wide", None),
        P("wide", "narrow"),
        P("wide", "narrow", None, None),
    )
    return jax.shard_map(
        functools.partial(on_device, mesh.shape["wide"]),
        mesh=mesh,
        in_specs=placed,
        out_specs=P("wide", "narrow", None),
        check_vma=False,
    )
```

```python
import functools

import jax
import jax.numpy as jnp
from jax import lax
from jax.experimental import pallas as pl
from jax.experimental.pallas import tpu as pltpu
from jax.sharding import PartitionSpec as P


def ladder_kernel(n_k, places_ref, recv_ref, blk_ref, out_ref):
    x = pl.program_id(0)
    acc = jnp.zeros(out_ref.shape[1:], jnp.float32)
    for k in range(n_k):
        tile = recv_ref[places_ref[x * n_k + k]]
        acc = acc + jnp.dot(tile, blk_ref[0, k], preferred_element_type=jnp.float32)
    out_ref[0] = acc.astype(out_ref.dtype)


def ladder(places, received, blocks):
    n_x, n_k, t, s = blocks.shape
    n_recv, rows, _ = received.shape
    grid_spec = pltpu.PrefetchScalarGridSpec(
        num_scalar_prefetch=1,
        grid=(n_x,),
        in_specs=[
            pl.BlockSpec((n_recv, rows, t), lambda x, p: (0, 0, 0)),
            pl.BlockSpec((1, n_k, t, s), lambda x, p: (x, 0, 0, 0)),
        ],
        out_specs=pl.BlockSpec((1, rows, s), lambda x, p: (x, 0, 0)),
    )
    return pl.pallas_call(
        functools.partial(ladder_kernel, n_k),
        out_shape=jax.ShapeDtypeStruct((n_x, rows, s), jnp.bfloat16),
        grid_spec=grid_spec,
        cost_estimate=pl.CostEstimate(
            flops=2 * n_x * n_k * rows * t * s,
            transcendentals=0,
            bytes_accessed=2 * (received.size + blocks.size + n_x * rows * s),
        ),
    )(places.reshape(-1), received, blocks)


def on_device(amplitudes, send_list, tile_positions, integrals):
    outgoing = amplitudes[send_list[0]]
    received = lax.all_to_all(outgoing, "wide", split_axis=0, concat_axis=0, tiled=True)
    blocks = lax.all_gather(integrals, "narrow", axis=1, tiled=True)
    places = lax.all_gather(tile_positions, "narrow", axis=1, tiled=True)
    return ladder(places, received, blocks)


def solution(mesh):
    placed = (
        P("wide", "narrow", None),
        P("wide", None),
        P("wide", "narrow"),
        P("wide", "narrow", None, None),
    )
    return jax.shard_map(
        on_device, mesh=mesh, in_specs=placed, out_specs=P("wide", "narrow", None), check_vma=False
    )
```

```python
import functools

import jax
import jax.numpy as jnp
from jax import lax
from jax.experimental import pallas as pl
from jax.experimental.pallas import tpu as pltpu
from jax.sharding import PartitionSpec as P

MESH = pl.DeviceIdType.MESH


def gather_kernel(n_nar, src_ref, dst_ref, send_sem, recv_sem, local_sem):
    me = lax.axis_index("narrow")
    w = lax.axis_index("wide")

    barrier = pltpu.get_barrier_semaphore()
    for i in range(1, n_nar):
        peer = lax.rem(me + i, n_nar)
        pl.semaphore_signal(barrier, 1, device_id=(w, peer), device_id_type=MESH)
    pl.semaphore_wait(barrier, n_nar - 1)

    local = pltpu.make_async_copy(src_ref, dst_ref.at[me], local_sem)
    local.start()

    def remote(peer, slot):
        return pltpu.make_async_remote_copy(
            src_ref=src_ref,
            dst_ref=dst_ref.at[slot],
            send_sem=send_sem.at[peer],
            recv_sem=recv_sem.at[slot],
            device_id=(w, peer),
            device_id_type=MESH,
        )

    for i in range(1, n_nar):
        remote(lax.rem(me + i, n_nar), me).start()
    for i in range(1, n_nar):
        remote(lax.rem(me + i, n_nar), me).wait_send()
        owner = lax.rem(me + n_nar - i, n_nar)
        remote(owner, owner).wait_recv()
    local.wait()


def gather_integrals(integrals, n_nar):
    return pl.pallas_call(
        functools.partial(gather_kernel, n_nar),
        out_shape=jax.ShapeDtypeStruct((n_nar,) + integrals.shape, integrals.dtype),
        in_specs=[pl.BlockSpec(memory_space=pl.ANY)],
        out_specs=pl.BlockSpec(memory_space=pl.ANY),
        scratch_shapes=[
            pltpu.SemaphoreType.DMA((n_nar,)),
            pltpu.SemaphoreType.DMA((n_nar,)),
            pltpu.SemaphoreType.DMA,
        ],
        compiler_params=pltpu.CompilerParams(collective_id=0, has_side_effects=True),
        cost_estimate=pl.CostEstimate(
            flops=0, transcendentals=0, bytes_accessed=2 * n_nar * integrals.size * 2
        ),
    )(integrals)


def ladder_kernel(n_k, per, places_ref, recv_ref, blk_ref, out_ref):
    x = pl.program_id(0)
    tiles = [recv_ref[places_ref[x * n_k + k]] for k in range(n_k)]
    lhs = jnp.concatenate(tiles, axis=1)
    rhs = blk_ref[...].reshape(n_k * blk_ref.shape[-2], blk_ref.shape[-1])
    out_ref[0] = jnp.dot(lhs, rhs, preferred_element_type=jnp.float32).astype(out_ref.dtype)


def ladder(places, received, blocks):
    n_nar, n_x, per, t, s = blocks.shape
    n_k = n_nar * per
    n_recv, rows, _ = received.shape
    grid_spec = pltpu.PrefetchScalarGridSpec(
        num_scalar_prefetch=1,
        grid=(n_x,),
        in_specs=[
            pl.BlockSpec((n_recv, rows, t), lambda x, p: (0, 0, 0)),
            pl.BlockSpec((n_nar, 1, per, t, s), lambda x, p: (0, x, 0, 0, 0)),
        ],
        out_specs=pl.BlockSpec((1, rows, s), lambda x, p: (x, 0, 0)),
    )
    return pl.pallas_call(
        functools.partial(ladder_kernel, n_k, per),
        out_shape=jax.ShapeDtypeStruct((n_x, rows, s), jnp.bfloat16),
        grid_spec=grid_spec,
        cost_estimate=pl.CostEstimate(
            flops=2 * n_x * n_k * rows * t * s,
            transcendentals=0,
            bytes_accessed=2 * (received.size + blocks.size + n_x * rows * s),
        ),
    )(places.reshape(-1), received, blocks)


def on_device(n_nar, amplitudes, send_list, tile_positions, integrals):
    outgoing = amplitudes[send_list[0]]
    received = lax.all_to_all(outgoing, "wide", split_axis=0, concat_axis=0, tiled=True)
    blocks = gather_integrals(integrals, n_nar)
    places = lax.all_gather(tile_positions, "narrow", axis=1, tiled=True)
    return ladder(places, received, blocks)


def solution(mesh):
    placed = (
        P("wide", "narrow", None),
        P("wide", None),
        P("wide", "narrow"),
        P("wide", "narrow", None, None),
    )
    return jax.shard_map(
        functools.partial(on_device, mesh.shape["narrow"]),
        mesh=mesh,
        in_specs=placed,
        out_specs=P("wide", "narrow", None),
        check_vma=False,
    )
```

```python
import functools

import jax
import jax.numpy as jnp
from jax import lax
from jax.experimental import pallas as pl
from jax.experimental.pallas import tpu as pltpu
from jax.sharding import PartitionSpec as P

MESH = pl.DeviceIdType.MESH


def gather_kernel(n_nar, src_ref, dst_ref, send_sem, recv_sem, local_sem):
    me = lax.axis_index("narrow")
    w = lax.axis_index("wide")

    barrier = pltpu.get_barrier_semaphore()
    for i in range(1, n_nar):
        peer = lax.rem(me + i, n_nar)
        pl.semaphore_signal(barrier, 1, device_id=(w, peer), device_id_type=MESH)
    pl.semaphore_wait(barrier, n_nar - 1)

    local = pltpu.make_async_copy(src_ref, dst_ref.at[me], local_sem)
    local.start()

    def remote(peer, slot):
        return pltpu.make_async_remote_copy(
            src_ref=src_ref,
            dst_ref=dst_ref.at[slot],
            send_sem=send_sem.at[peer],
            recv_sem=recv_sem.at[slot],
            device_id=(w, peer),
            device_id_type=MESH,
        )

    for i in range(1, n_nar):
        remote(lax.rem(me + i, n_nar), me).start()
    for i in range(1, n_nar):
        remote(lax.rem(me + i, n_nar), me).wait_send()
        owner = lax.rem(me + n_nar - i, n_nar)
        remote(owner, owner).wait_recv()
    local.wait()


def gather_integrals(integrals, n_nar):
    return pl.pallas_call(
        functools.partial(gather_kernel, n_nar),
        out_shape=jax.ShapeDtypeStruct((n_nar,) + integrals.shape, integrals.dtype),
        in_specs=[pl.BlockSpec(memory_space=pl.ANY)],
        out_specs=pl.BlockSpec(memory_space=pl.ANY),
        scratch_shapes=[
            pltpu.SemaphoreType.DMA((n_nar,)),
            pltpu.SemaphoreType.DMA((n_nar,)),
            pltpu.SemaphoreType.DMA,
        ],
        compiler_params=pltpu.CompilerParams(collective_id=0, has_side_effects=True),
        cost_estimate=pl.CostEstimate(
            flops=0, transcendentals=0, bytes_accessed=2 * n_nar * integrals.size * 2
        ),
    )(integrals)


def ladder_kernel(n_x, n_k, places_ref, recv_hbm, blk_hbm, out_ref, tiles, blks, sems):
    def copies(x, slot):
        picked = [
            pltpu.make_async_copy(recv_hbm.at[places_ref[x * n_k + k]], tiles.at[slot, k], sems.at[slot, k])
            for k in range(n_k)
        ]
        return picked + [pltpu.make_async_copy(blk_hbm.at[:, x], blks.at[slot], sems.at[slot, n_k])]

    for c in copies(0, 0):
        c.start()
    for x in range(n_x):
        slot = x % 2
        if x + 1 < n_x:
            for c in copies(x + 1, 1 - slot):
                c.start()
        for c in copies(x, slot):
            c.wait()
        lhs = jnp.concatenate([tiles[slot, k] for k in range(n_k)], axis=1)
        rhs = blks[slot].reshape(n_k * blks.shape[-2], blks.shape[-1])
        out_ref[x] = jnp.dot(lhs, rhs, preferred_element_type=jnp.float32).astype(out_ref.dtype)


def ladder(places, received, blocks):
    n_nar, n_x, per, t, s = blocks.shape
    n_k = n_nar * per
    n_recv, rows, _ = received.shape
    return pl.pallas_call(
        functools.partial(ladder_kernel, n_x, n_k),
        out_shape=jax.ShapeDtypeStruct((n_x, rows, s), jnp.bfloat16),
        in_specs=[
            pl.BlockSpec(memory_space=pltpu.SMEM),
            pl.BlockSpec(memory_space=pl.ANY),
            pl.BlockSpec(memory_space=pl.ANY),
        ],
        out_specs=pl.BlockSpec(memory_space=pltpu.VMEM),
        scratch_shapes=[
            pltpu.VMEM((2, n_k, rows, t), received.dtype),
            pltpu.VMEM((2, n_nar, per, t, s), blocks.dtype),
            pltpu.SemaphoreType.DMA((2, n_k + 1)),
        ],
        cost_estimate=pl.CostEstimate(
            flops=2 * n_x * n_k * rows * t * s,
            transcendentals=0,
            bytes_accessed=2 * (2 * blocks.size + n_x * rows * s),
        ),
    )(places.reshape(-1), received, blocks)


def on_device(n_nar, amplitudes, send_list, tile_positions, integrals):
    outgoing = amplitudes[send_list[0]]
    received = lax.all_to_all(outgoing, "wide", split_axis=0, concat_axis=0, tiled=True)
    blocks = gather_integrals(integrals, n_nar)
    places = lax.all_gather(tile_positions, "narrow", axis=1, tiled=True)
    return ladder(places, received, blocks)


def solution(mesh):
    placed = (
        P("wide", "narrow", None),
        P("wide", None),
        P("wide", "narrow"),
        P("wide", "narrow", None, None),
    )
    return jax.shard_map(
        functools.partial(on_device, mesh.shape["narrow"]),
        mesh=mesh,
        in_specs=placed,
        out_specs=P("wide", "narrow", None),
        check_vma=False,
    )
```

```python
import functools

import jax
import jax.numpy as jnp
from jax import lax
from jax.experimental import pallas as pl
from jax.experimental.pallas import tpu as pltpu
from jax.sharding import PartitionSpec as P

MESH = pl.DeviceIdType.MESH


def gather_kernel(n_nar, src_ref, dst_ref, send_sem, recv_sem, local_sem):
    me = lax.axis_index("narrow")
    w = lax.axis_index("wide")

    barrier = pltpu.get_barrier_semaphore()
    for i in range(1, n_nar):
        peer = lax.rem(me + i, n_nar)
        pl.semaphore_signal(barrier, 1, device_id=(w, peer), device_id_type=MESH)
    pl.semaphore_wait(barrier, n_nar - 1)

    local = pltpu.make_async_copy(src_ref, dst_ref.at[me], local_sem)
    local.start()

    def remote(peer, slot):
        return pltpu.make_async_remote_copy(
            src_ref=src_ref,
            dst_ref=dst_ref.at[slot],
            send_sem=send_sem.at[peer],
            recv_sem=recv_sem.at[slot],
            device_id=(w, peer),
            device_id_type=MESH,
        )

    for i in range(1, n_nar):
        remote(lax.rem(me + i, n_nar), me).start()
    for i in range(1, n_nar):
        remote(lax.rem(me + i, n_nar), me).wait_send()
        owner = lax.rem(me + n_nar - i, n_nar)
        remote(owner, owner).wait_recv()
    local.wait()


def gather_integrals(integrals, n_nar):
    return pl.pallas_call(
        functools.partial(gather_kernel, n_nar),
        out_shape=jax.ShapeDtypeStruct((n_nar,) + integrals.shape, integrals.dtype),
        in_specs=[pl.BlockSpec(memory_space=pl.ANY)],
        out_specs=pl.BlockSpec(memory_space=pl.ANY),
        scratch_shapes=[
            pltpu.SemaphoreType.DMA((n_nar,)),
            pltpu.SemaphoreType.DMA((n_nar,)),
            pltpu.SemaphoreType.DMA,
        ],
        compiler_params=pltpu.CompilerParams(collective_id=0, has_side_effects=True),
        cost_estimate=pl.CostEstimate(
            flops=0, transcendentals=0, bytes_accessed=2 * n_nar * integrals.size * 2
        ),
    )(integrals)


def ladder_kernel(n_x, n_k, places_ref, recv_hbm, blk_hbm, out_ref, tiles, blks, sems):
    def copies(x, slot):
        picked = [
            pltpu.make_async_copy(recv_hbm.at[places_ref[x * n_k + k]], tiles.at[slot, k], sems.at[slot, k])
            for k in range(n_k)
        ]
        return picked + [pltpu.make_async_copy(blk_hbm.at[:, x], blks.at[slot], sems.at[slot, n_k])]

    for c in copies(0, 0):
        c.start()
    for x in range(n_x):
        slot = x % 2
        if x + 1 < n_x:
            for c in copies(x + 1, 1 - slot):
                c.start()
        for c in copies(x, slot):
            c.wait()
        lhs = jnp.concatenate([tiles[slot, k] for k in range(n_k)], axis=1)
        rhs = blks[slot].reshape(n_k * blks.shape[-2], blks.shape[-1])
        out_ref[x] = jnp.dot(lhs, rhs, preferred_element_type=jnp.float32).astype(out_ref.dtype)


def ladder(places, received, blocks):
    n_nar, n_x, per, t, s = blocks.shape
    n_k = n_nar * per
    n_recv, rows, _ = received.shape
    return pl.pallas_call(
        functools.partial(ladder_kernel, n_x, n_k),
        out_shape=jax.ShapeDtypeStruct((n_x, rows, s), jnp.bfloat16),
        in_specs=[
            pl.BlockSpec(memory_space=pltpu.SMEM),
            pl.BlockSpec(memory_space=pl.ANY),
            pl.BlockSpec(memory_space=pl.ANY),
        ],
        out_specs=pl.BlockSpec(memory_space=pltpu.VMEM),
        scratch_shapes=[
            pltpu.VMEM((2, n_k, rows, t), received.dtype),
            pltpu.VMEM((2, n_nar, per, t, s), blocks.dtype),
            pltpu.SemaphoreType.DMA((2, n_k + 1)),
        ],
        cost_estimate=pl.CostEstimate(
            flops=2 * n_x * n_k * rows * t * s,
            transcendentals=0,
            bytes_accessed=2 * (2 * blocks.size + n_x * rows * s),
        ),
    )(places.reshape(-1), received, blocks)


def pick_kernel(n_out, sel_ref, amp_ref, out_hbm, sems):
    copies = [pltpu.make_async_copy(amp_ref.at[sel_ref[j]], out_hbm.at[j], sems.at[j]) for j in range(n_out)]
    for c in copies:
        c.start()
    for c in copies:
        c.wait()


def pick_outgoing(amplitudes, selection):
    n_out = selection.shape[0]
    return pl.pallas_call(
        functools.partial(pick_kernel, n_out),
        out_shape=jax.ShapeDtypeStruct((n_out,) + amplitudes.shape[1:], amplitudes.dtype),
        in_specs=[pl.BlockSpec(memory_space=pltpu.SMEM), pl.BlockSpec(memory_space=pltpu.VMEM)],
        out_specs=pl.BlockSpec(memory_space=pl.ANY),
        scratch_shapes=[pltpu.SemaphoreType.DMA((n_out,))],
        cost_estimate=pl.CostEstimate(flops=0, transcendentals=0, bytes_accessed=4 * n_out * amplitudes[0].size),
    )(selection, amplitudes)


def on_device(n_nar, amplitudes, send_list, tile_positions, integrals):
    outgoing = pick_outgoing(amplitudes, send_list[0])
    received = lax.all_to_all(outgoing, "wide", split_axis=0, concat_axis=0, tiled=True)
    blocks = gather_integrals(integrals, n_nar)
    places = lax.all_gather(tile_positions, "narrow", axis=1, tiled=True)
    return ladder(places, received, blocks)


def solution(mesh):
    placed = (
        P("wide", "narrow", None),
        P("wide", None),
        P("wide", "narrow"),
        P("wide", "narrow", None, None),
    )
    return jax.shard_map(
        functools.partial(on_device, mesh.shape["narrow"]),
        mesh=mesh,
        in_specs=placed,
        out_specs=P("wide", "narrow", None),
        check_vma=False,
    )
```

```python
import functools

import jax
import jax.numpy as jnp
from jax import lax
from jax.experimental import pallas as pl
from jax.experimental.pallas import tpu as pltpu
from jax.sharding import PartitionSpec as P

MESH = pl.DeviceIdType.MESH
CUT = 64


def gather_kernel(n_nar, src_ref, dst_ref, send_sem, recv_sem, local_sem):
    me = lax.axis_index("narrow")
    w = lax.axis_index("wide")

    barrier = pltpu.get_barrier_semaphore()
    for i in range(1, n_nar):
        peer = lax.rem(me + i, n_nar)
        pl.semaphore_signal(barrier, 1, device_id=(w, peer), device_id_type=MESH)
    pl.semaphore_wait(barrier, n_nar - 1)

    local = pltpu.make_async_copy(src_ref, dst_ref.at[me], local_sem)
    local.start()

    def remote(peer, slot):
        return pltpu.make_async_remote_copy(
            src_ref=src_ref,
            dst_ref=dst_ref.at[slot],
            send_sem=send_sem.at[peer],
            recv_sem=recv_sem.at[slot],
            device_id=(w, peer),
            device_id_type=MESH,
        )

    for i in range(1, n_nar):
        remote(lax.rem(me + i, n_nar), me).start()
    for i in range(1, n_nar):
        remote(lax.rem(me + i, n_nar), me).wait_send()
        owner = lax.rem(me + n_nar - i, n_nar)
        remote(owner, owner).wait_recv()
    local.wait()


def gather_integrals(integrals, n_nar):
    return pl.pallas_call(
        functools.partial(gather_kernel, n_nar),
        out_shape=jax.ShapeDtypeStruct((n_nar,) + integrals.shape, integrals.dtype),
        in_specs=[pl.BlockSpec(memory_space=pl.ANY)],
        out_specs=pl.BlockSpec(memory_space=pl.ANY),
        scratch_shapes=[
            pltpu.SemaphoreType.DMA((n_nar,)),
            pltpu.SemaphoreType.DMA((n_nar,)),
            pltpu.SemaphoreType.DMA,
        ],
        compiler_params=pltpu.CompilerParams(collective_id=0, has_side_effects=True),
        cost_estimate=pl.CostEstimate(
            flops=0, transcendentals=0, bytes_accessed=2 * n_nar * integrals.size * 2
        ),
    )(integrals)


def ladder_kernel(n_x, n_k, places_ref, head_hbm, tail_hbm, blk_hbm, out_ref, tiles, blks, sems):
    def copies(x, slot):
        cut = head_hbm.shape[1]
        picked = []
        for k in range(n_k):
            p = places_ref[x * n_k + k]
            dst = tiles.at[slot, k]
            picked.append(pltpu.make_async_copy(head_hbm.at[p], dst.at[pl.ds(0, cut)], sems.at[slot, 0, k]))
            picked.append(
                pltpu.make_async_copy(tail_hbm.at[p], dst.at[pl.ds(cut, dst.shape[0] - cut)], sems.at[slot, 1, k])
            )
        return picked + [pltpu.make_async_copy(blk_hbm.at[:, x], blks.at[slot], sems.at[slot, 2, 0])]

    for c in copies(0, 0):
        c.start()
    for x in range(n_x):
        slot = x % 2
        if x + 1 < n_x:
            for c in copies(x + 1, 1 - slot):
                c.start()
        for c in copies(x, slot):
            c.wait()
        lhs = jnp.concatenate([tiles[slot, k] for k in range(n_k)], axis=1)
        rhs = blks[slot].reshape(n_k * blks.shape[-2], blks.shape[-1])
        out_ref[x] = jnp.dot(lhs, rhs, preferred_element_type=jnp.float32).astype(out_ref.dtype)


def ladder(places, head, tail, blocks):
    n_nar, n_x, per, t, s = blocks.shape
    n_k = n_nar * per
    rows = head.shape[1] + tail.shape[1]
    return pl.pallas_call(
        functools.partial(ladder_kernel, n_x, n_k),
        out_shape=jax.ShapeDtypeStruct((n_x, rows, s), jnp.bfloat16),
        in_specs=[
            pl.BlockSpec(memory_space=pltpu.SMEM),
            pl.BlockSpec(memory_space=pl.ANY),
            pl.BlockSpec(memory_space=pl.ANY),
            pl.BlockSpec(memory_space=pl.ANY),
        ],
        out_specs=pl.BlockSpec(memory_space=pltpu.VMEM),
        scratch_shapes=[
            pltpu.VMEM((2, n_k, rows, t), head.dtype),
            pltpu.VMEM((2, n_nar, per, t, s), blocks.dtype),
            pltpu.SemaphoreType.DMA((2, 3, n_k)),
        ],
        cost_estimate=pl.CostEstimate(
            flops=2 * n_x * n_k * rows * t * s,
            transcendentals=0,
            bytes_accessed=2 * (2 * blocks.size + n_x * rows * s),
        ),
    )(places.reshape(-1), head, tail, blocks)


def pick_kernel(n_out, cut, sel_ref, amp_ref, head_hbm, tail_hbm, sems):
    copies = []
    for j in range(n_out):
        src = amp_ref.at[sel_ref[j]]
        copies.append(pltpu.make_async_copy(src.at[pl.ds(0, cut)], head_hbm.at[j], sems.at[0, j]))
        copies.append(pltpu.make_async_copy(src.at[pl.ds(cut, src.shape[0] - cut)], tail_hbm.at[j], sems.at[1, j]))
    for c in copies:
        c.start()
    for c in copies:
        c.wait()


def pick_outgoing(amplitudes, selection, cut):
    n_out, (rows, t) = selection.shape[0], amplitudes.shape[1:]
    return pl.pallas_call(
        functools.partial(pick_kernel, n_out, cut),
        out_shape=(
            jax.ShapeDtypeStruct((n_out, cut, t), amplitudes.dtype),
            jax.ShapeDtypeStruct((n_out, rows - cut, t), amplitudes.dtype),
        ),
        in_specs=[pl.BlockSpec(memory_space=pltpu.SMEM), pl.BlockSpec(memory_space=pltpu.VMEM)],
        out_specs=(pl.BlockSpec(memory_space=pl.ANY), pl.BlockSpec(memory_space=pl.ANY)),
        scratch_shapes=[pltpu.SemaphoreType.DMA((2, n_out))],
        cost_estimate=pl.CostEstimate(flops=0, transcendentals=0, bytes_accessed=4 * n_out * amplitudes[0].size),
    )(selection, amplitudes)


def on_device(n_nar, amplitudes, send_list, tile_positions, integrals):
    head, tail = pick_outgoing(amplitudes, send_list[0], CUT)
    head = lax.all_to_all(head, "wide", split_axis=0, concat_axis=0, tiled=True)
    tail = lax.all_to_all(tail, "wide", split_axis=0, concat_axis=0, tiled=True)
    blocks = gather_integrals(integrals, n_nar)
    places = lax.all_gather(tile_positions, "narrow", axis=1, tiled=True)
    return ladder(places, head, tail, blocks)


def solution(mesh):
    placed = (
        P("wide", "narrow", None),
        P("wide", None),
        P("wide", "narrow"),
        P("wide", "narrow", None, None),
    )
    return jax.shard_map(
        functools.partial(on_device, mesh.shape["narrow"]),
        mesh=mesh,
        in_specs=placed,
        out_specs=P("wide", "narrow", None),
        check_vma=False,
    )
```

```python
import functools

import jax
import jax.numpy as jnp
from jax import lax
from jax.experimental import pallas as pl
from jax.experimental.pallas import tpu as pltpu
from jax.sharding import PartitionSpec as P

MESH = pl.DeviceIdType.MESH
CUT = 64


def gather_kernel(n_nar, src_ref, pos_ref, dst_ref, pos_dst, send_sem, recv_sem, local_sem):
    me = lax.axis_index("narrow")
    w = lax.axis_index("wide")

    barrier = pltpu.get_barrier_semaphore()
    for i in range(1, n_nar):
        peer = lax.rem(me + i, n_nar)
        pl.semaphore_signal(barrier, 1, device_id=(w, peer), device_id_type=MESH)
    pl.semaphore_wait(barrier, n_nar - 1)

    locals_ = [
        pltpu.make_async_copy(src_ref, dst_ref.at[me], local_sem.at[0]),
        pltpu.make_async_copy(pos_ref, pos_dst.at[me], local_sem.at[1]),
    ]
    for c in locals_:
        c.start()

    def remote(peer, slot):
        return [
            pltpu.make_async_remote_copy(
                src_ref=s,
                dst_ref=d.at[slot],
                send_sem=send_sem.at[part, peer],
                recv_sem=recv_sem.at[part, slot],
                device_id=(w, peer),
                device_id_type=MESH,
            )
            for part, (s, d) in enumerate(((src_ref, dst_ref), (pos_ref, pos_dst)))
        ]

    for i in range(1, n_nar):
        for c in remote(lax.rem(me + i, n_nar), me):
            c.start()
    for i in range(1, n_nar):
        for c in remote(lax.rem(me + i, n_nar), me):
            c.wait_send()
        owner = lax.rem(me + n_nar - i, n_nar)
        for c in remote(owner, owner):
            c.wait_recv()
    for c in locals_:
        c.wait()


def gather_integrals(integrals, positions, n_nar):
    return pl.pallas_call(
        functools.partial(gather_kernel, n_nar),
        out_shape=(
            jax.ShapeDtypeStruct((n_nar,) + integrals.shape, integrals.dtype),
            jax.ShapeDtypeStruct((n_nar,) + positions.shape, positions.dtype),
        ),
        in_specs=[pl.BlockSpec(memory_space=pl.ANY), pl.BlockSpec(memory_space=pl.ANY)],
        out_specs=(pl.BlockSpec(memory_space=pl.ANY), pl.BlockSpec(memory_space=pl.ANY)),
        scratch_shapes=[
            pltpu.SemaphoreType.DMA((2, n_nar)),
            pltpu.SemaphoreType.DMA((2, n_nar)),
            pltpu.SemaphoreType.DMA((2,)),
        ],
        compiler_params=pltpu.CompilerParams(collective_id=0, has_side_effects=True),
        cost_estimate=pl.CostEstimate(
            flops=0, transcendentals=0, bytes_accessed=2 * n_nar * integrals.size * 2
        ),
    )(integrals, positions)


def ladder_kernel(n_x, n_k, per, places_ref, head_hbm, tail_hbm, blk_hbm, out_ref, tiles, blks, sems):
    def copies(x, slot):
        cut = head_hbm.shape[1]
        picked = []
        for k in range(n_k):
            p = places_ref[k // per, x, k % per]
            dst = tiles.at[slot, k]
            picked.append(pltpu.make_async_copy(head_hbm.at[p], dst.at[pl.ds(0, cut)], sems.at[slot, 0, k]))
            picked.append(
                pltpu.make_async_copy(tail_hbm.at[p], dst.at[pl.ds(cut, dst.shape[0] - cut)], sems.at[slot, 1, k])
            )
        return picked + [pltpu.make_async_copy(blk_hbm.at[:, x], blks.at[slot], sems.at[slot, 2, 0])]

    for c in copies(0, 0):
        c.start()
    for x in range(n_x):
        slot = x % 2
        if x + 1 < n_x:
            for c in copies(x + 1, 1 - slot):
                c.start()
        for c in copies(x, slot):
            c.wait()
        lhs = jnp.concatenate([tiles[slot, k] for k in range(n_k)], axis=1)
        rhs = blks[slot].reshape(n_k * blks.shape[-2], blks.shape[-1])
        out_ref[x] = jnp.dot(lhs, rhs, preferred_element_type=jnp.float32).astype(out_ref.dtype)


def ladder(places, head, tail, blocks):
    n_nar, n_x, per, t, s = blocks.shape
    n_k = n_nar * per
    rows = head.shape[1] + tail.shape[1]
    return pl.pallas_call(
        functools.partial(ladder_kernel, n_x, n_k, per),
        out_shape=jax.ShapeDtypeStruct((n_x, rows, s), jnp.bfloat16),
        in_specs=[
            pl.BlockSpec(memory_space=pltpu.SMEM),
            pl.BlockSpec(memory_space=pl.ANY),
            pl.BlockSpec(memory_space=pl.ANY),
            pl.BlockSpec(memory_space=pl.ANY),
        ],
        out_specs=pl.BlockSpec(memory_space=pltpu.VMEM),
        scratch_shapes=[
            pltpu.VMEM((2, n_k, rows, t), head.dtype),
            pltpu.VMEM((2, n_nar, per, t, s), blocks.dtype),
            pltpu.SemaphoreType.DMA((2, 3, n_k)),
        ],
        cost_estimate=pl.CostEstimate(
            flops=2 * n_x * n_k * rows * t * s,
            transcendentals=0,
            bytes_accessed=2 * (2 * blocks.size + n_x * rows * s),
        ),
    )(places, head, tail, blocks)


def pick_kernel(n_out, cut, sel_ref, amp_ref, head_hbm, tail_hbm, sems):
    copies = []
    for j in range(n_out):
        src = amp_ref.at[sel_ref[j]]
        copies.append(pltpu.make_async_copy(src.at[pl.ds(0, cut)], head_hbm.at[j], sems.at[0, j]))
        copies.append(pltpu.make_async_copy(src.at[pl.ds(cut, src.shape[0] - cut)], tail_hbm.at[j], sems.at[1, j]))
    for c in copies:
        c.start()
    for c in copies:
        c.wait()


def pick_outgoing(amplitudes, selection, cut):
    n_out, (rows, t) = selection.shape[0], amplitudes.shape[1:]
    return pl.pallas_call(
        functools.partial(pick_kernel, n_out, cut),
        out_shape=(
            jax.ShapeDtypeStruct((n_out, cut, t), amplitudes.dtype),
            jax.ShapeDtypeStruct((n_out, rows - cut, t), amplitudes.dtype),
        ),
        in_specs=[pl.BlockSpec(memory_space=pltpu.SMEM), pl.BlockSpec(memory_space=pltpu.VMEM)],
        out_specs=(pl.BlockSpec(memory_space=pl.ANY), pl.BlockSpec(memory_space=pl.ANY)),
        scratch_shapes=[pltpu.SemaphoreType.DMA((2, n_out))],
        cost_estimate=pl.CostEstimate(flops=0, transcendentals=0, bytes_accessed=4 * n_out * amplitudes[0].size),
    )(selection, amplitudes)


def on_device(n_nar, amplitudes, send_list, tile_positions, integrals):
    head, tail = pick_outgoing(amplitudes, send_list[0], CUT)
    head = lax.all_to_all(head, "wide", split_axis=0, concat_axis=0, tiled=True)
    tail = lax.all_to_all(tail, "wide", split_axis=0, concat_axis=0, tiled=True)
    lanes = jnp.zeros((tile_positions.shape[0], 128), tile_positions.dtype)
    lanes = lax.dynamic_update_slice(lanes, tile_positions, (0, 0))
    blocks, places = gather_integrals(integrals, lanes, n_nar)
    return ladder(places, head, tail, blocks)


def solution(mesh):
    placed = (
        P("wide", "narrow", None),
        P("wide", None),
        P("wide", "narrow"),
        P("wide", "narrow", None, None),
    )
    return jax.shard_map(
        functools.partial(on_device, mesh.shape["narrow"]),
        mesh=mesh,
        in_specs=placed,
        out_specs=P("wide", "narrow", None),
        check_vma=False,
    )
```

```python
import functools

import jax
import jax.numpy as jnp
from jax import lax
from jax.experimental import pallas as pl
from jax.experimental.pallas import tpu as pltpu
from jax.sharding import PartitionSpec as P

MESH = pl.DeviceIdType.MESH
CUT = 48


def gather_kernel(n_nar, src_ref, pos_ref, dst_ref, pos_dst, send_sem, recv_sem, local_sem):
    me = lax.axis_index("narrow")
    w = lax.axis_index("wide")

    barrier = pltpu.get_barrier_semaphore()
    for i in range(1, n_nar):
        peer = lax.rem(me + i, n_nar)
        pl.semaphore_signal(barrier, 1, device_id=(w, peer), device_id_type=MESH)
    pl.semaphore_wait(barrier, n_nar - 1)

    locals_ = [
        pltpu.make_async_copy(src_ref, dst_ref.at[me], local_sem.at[0]),
        pltpu.make_async_copy(pos_ref, pos_dst.at[me], local_sem.at[1]),
    ]
    for c in locals_:
        c.start()

    def remote(peer, slot):
        return [
            pltpu.make_async_remote_copy(
                src_ref=s,
                dst_ref=d.at[slot],
                send_sem=send_sem.at[part, peer],
                recv_sem=recv_sem.at[part, slot],
                device_id=(w, peer),
                device_id_type=MESH,
            )
            for part, (s, d) in enumerate(((src_ref, dst_ref), (pos_ref, pos_dst)))
        ]

    for i in range(1, n_nar):
        for c in remote(lax.rem(me + i, n_nar), me):
            c.start()
    for i in range(1, n_nar):
        for c in remote(lax.rem(me + i, n_nar), me):
            c.wait_send()
        owner = lax.rem(me + n_nar - i, n_nar)
        for c in remote(owner, owner):
            c.wait_recv()
    for c in locals_:
        c.wait()


def gather_integrals(integrals, positions, n_nar):
    return pl.pallas_call(
        functools.partial(gather_kernel, n_nar),
        out_shape=(
            jax.ShapeDtypeStruct((n_nar,) + integrals.shape, integrals.dtype),
            jax.ShapeDtypeStruct((n_nar,) + positions.shape, positions.dtype),
        ),
        in_specs=[pl.BlockSpec(memory_space=pl.ANY), pl.BlockSpec(memory_space=pl.ANY)],
        out_specs=(pl.BlockSpec(memory_space=pl.ANY), pl.BlockSpec(memory_space=pl.ANY)),
        scratch_shapes=[
            pltpu.SemaphoreType.DMA((2, n_nar)),
            pltpu.SemaphoreType.DMA((2, n_nar)),
            pltpu.SemaphoreType.DMA((2,)),
        ],
        compiler_params=pltpu.CompilerParams(collective_id=0, has_side_effects=True),
        cost_estimate=pl.CostEstimate(
            flops=0, transcendentals=0, bytes_accessed=2 * n_nar * integrals.size * 2
        ),
    )(integrals, positions)


def ladder_kernel(n_x, n_k, per, places_ref, head_hbm, tail_hbm, blk_hbm, out_ref, tiles, blks, sems):
    def copies(x, slot):
        cut = head_hbm.shape[1]
        picked = []
        for k in range(n_k):
            p = places_ref[k // per, x, k % per]
            dst = tiles.at[slot, k]
            picked.append(pltpu.make_async_copy(head_hbm.at[p], dst.at[pl.ds(0, cut)], sems.at[slot, 0, k]))
            picked.append(
                pltpu.make_async_copy(tail_hbm.at[p], dst.at[pl.ds(cut, dst.shape[0] - cut)], sems.at[slot, 1, k])
            )
        return picked + [pltpu.make_async_copy(blk_hbm.at[:, x], blks.at[slot], sems.at[slot, 2, 0])]

    for c in copies(0, 0):
        c.start()
    for x in range(n_x):
        slot = x % 2
        if x + 1 < n_x:
            for c in copies(x + 1, 1 - slot):
                c.start()
        for c in copies(x, slot):
            c.wait()
        lhs = jnp.concatenate([tiles[slot, k] for k in range(n_k)], axis=1)
        rhs = blks[slot].reshape(n_k * blks.shape[-2], blks.shape[-1])
        out_ref[x] = jnp.dot(lhs, rhs, preferred_element_type=jnp.float32).astype(out_ref.dtype)


def ladder(places, head, tail, blocks):
    n_nar, n_x, per, t, s = blocks.shape
    n_k = n_nar * per
    rows = head.shape[1] + tail.shape[1]
    return pl.pallas_call(
        functools.partial(ladder_kernel, n_x, n_k, per),
        out_shape=jax.ShapeDtypeStruct((n_x, rows, s), jnp.bfloat16),
        in_specs=[
            pl.BlockSpec(memory_space=pltpu.SMEM),
            pl.BlockSpec(memory_space=pl.ANY),
            pl.BlockSpec(memory_space=pl.ANY),
            pl.BlockSpec(memory_space=pl.ANY),
        ],
        out_specs=pl.BlockSpec(memory_space=pltpu.VMEM),
        scratch_shapes=[
            pltpu.VMEM((2, n_k, rows, t), head.dtype),
            pltpu.VMEM((2, n_nar, per, t, s), blocks.dtype),
            pltpu.SemaphoreType.DMA((2, 3, n_k)),
        ],
        cost_estimate=pl.CostEstimate(
            flops=2 * n_x * n_k * rows * t * s,
            transcendentals=0,
            bytes_accessed=2 * (2 * blocks.size + n_x * rows * s),
        ),
    )(places, head, tail, blocks)


def pick_kernel(n_out, cut, sel_ref, amp_ref, head_hbm, tail_hbm, sems):
    copies = []
    for j in range(n_out):
        src = amp_ref.at[sel_ref[j]]
        copies.append(pltpu.make_async_copy(src.at[pl.ds(0, cut)], head_hbm.at[j], sems.at[0, j]))
        copies.append(pltpu.make_async_copy(src.at[pl.ds(cut, src.shape[0] - cut)], tail_hbm.at[j], sems.at[1, j]))
    for c in copies:
        c.start()
    for c in copies:
        c.wait()


def pick_outgoing(amplitudes, selection, cut):
    n_out, (rows, t) = selection.shape[0], amplitudes.shape[1:]
    return pl.pallas_call(
        functools.partial(pick_kernel, n_out, cut),
        out_shape=(
            jax.ShapeDtypeStruct((n_out, cut, t), amplitudes.dtype),
            jax.ShapeDtypeStruct((n_out, rows - cut, t), amplitudes.dtype),
        ),
        in_specs=[pl.BlockSpec(memory_space=pltpu.SMEM), pl.BlockSpec(memory_space=pltpu.VMEM)],
        out_specs=(pl.BlockSpec(memory_space=pl.ANY), pl.BlockSpec(memory_space=pl.ANY)),
        scratch_shapes=[pltpu.SemaphoreType.DMA((2, n_out))],
        cost_estimate=pl.CostEstimate(flops=0, transcendentals=0, bytes_accessed=4 * n_out * amplitudes[0].size),
    )(selection, amplitudes)


def on_device(n_nar, amplitudes, send_list, tile_positions, integrals):
    head, tail = pick_outgoing(amplitudes, send_list[0], CUT)
    head = lax.all_to_all(head, "wide", split_axis=0, concat_axis=0, tiled=True)
    tail = lax.all_to_all(tail, "wide", split_axis=0, concat_axis=0, tiled=True)
    lanes = jnp.zeros((tile_positions.shape[0], 128), tile_positions.dtype)
    lanes = lax.dynamic_update_slice(lanes, tile_positions, (0, 0))
    blocks, places = gather_integrals(integrals, lanes, n_nar)
    return ladder(places, head, tail, blocks)


def solution(mesh):
    placed = (
        P("wide", "narrow", None),
        P("wide", None),
        P("wide", "narrow"),
        P("wide", "narrow", None, None),
    )
    return jax.shard_map(
        functools.partial(on_device, mesh.shape["narrow"]),
        mesh=mesh,
        in_specs=placed,
        out_specs=P("wide", "narrow", None),
        check_vma=False,
    )
```

```python
import functools

import jax
import jax.numpy as jnp
from jax import lax
from jax.experimental import pallas as pl
from jax.experimental.pallas import tpu as pltpu
from jax.sharding import PartitionSpec as P

MESH = pl.DeviceIdType.MESH
CUT = 48


def gather_kernel(n_nar, src_ref, pos_ref, dst_ref, pos_dst, send_sem, recv_sem, local_sem):
    me = lax.axis_index("narrow")
    w = lax.axis_index("wide")

    barrier = pltpu.get_barrier_semaphore()
    for i in range(1, n_nar):
        peer = lax.rem(me + i, n_nar)
        pl.semaphore_signal(barrier, 1, device_id=(w, peer), device_id_type=MESH)
    pl.semaphore_wait(barrier, n_nar - 1)

    locals_ = [
        pltpu.make_async_copy(src_ref, dst_ref.at[me], local_sem.at[0]),
        pltpu.make_async_copy(pos_ref, pos_dst.at[me], local_sem.at[1]),
    ]
    for c in locals_:
        c.start()

    def remote(peer, slot):
        return [
            pltpu.make_async_remote_copy(
                src_ref=s,
                dst_ref=d.at[slot],
                send_sem=send_sem.at[part, peer],
                recv_sem=recv_sem.at[part, slot],
                device_id=(w, peer),
                device_id_type=MESH,
            )
            for part, (s, d) in enumerate(((src_ref, dst_ref), (pos_ref, pos_dst)))
        ]

    for i in range(1, n_nar):
        for c in remote(lax.rem(me + i, n_nar), me):
            c.start()
    for i in range(1, n_nar):
        for c in remote(lax.rem(me + i, n_nar), me):
            c.wait_send()
        owner = lax.rem(me + n_nar - i, n_nar)
        for c in remote(owner, owner):
            c.wait_recv()
    for c in locals_:
        c.wait()


def gather_integrals(integrals, positions, n_nar):
    return pl.pallas_call(
        functools.partial(gather_kernel, n_nar),
        out_shape=(
            jax.ShapeDtypeStruct((n_nar,) + integrals.shape, integrals.dtype),
            jax.ShapeDtypeStruct((n_nar,) + positions.shape, positions.dtype),
        ),
        in_specs=[pl.BlockSpec(memory_space=pl.ANY), pl.BlockSpec(memory_space=pl.ANY)],
        out_specs=(pl.BlockSpec(memory_space=pl.ANY), pl.BlockSpec(memory_space=pl.ANY)),
        scratch_shapes=[
            pltpu.SemaphoreType.DMA((2, n_nar)),
            pltpu.SemaphoreType.DMA((2, n_nar)),
            pltpu.SemaphoreType.DMA((2,)),
        ],
        compiler_params=pltpu.CompilerParams(collective_id=0, has_side_effects=True),
        cost_estimate=pl.CostEstimate(
            flops=0, transcendentals=0, bytes_accessed=2 * n_nar * integrals.size * 2
        ),
    )(integrals, positions)


def ladder_kernel(n_x, n_k, per, places_ref, head_hbm, tail_hbm, blk_hbm, out_ref, tiles, blks, sems):
    def copies(x, slot):
        cut = head_hbm.shape[1]
        picked = []
        for k in range(n_k):
            p = places_ref[k // per, x, k % per]
            dst = tiles.at[slot, k]
            picked.append(pltpu.make_async_copy(head_hbm.at[p], dst.at[pl.ds(0, cut)], sems.at[slot, 0, k]))
            picked.append(
                pltpu.make_async_copy(tail_hbm.at[p], dst.at[pl.ds(cut, dst.shape[0] - cut)], sems.at[slot, 1, k])
            )
        return picked + [pltpu.make_async_copy(blk_hbm.at[:, x], blks.at[slot], sems.at[slot, 2, 0])]

    for c in copies(0, 0):
        c.start()
    for x in range(n_x):
        slot = x % 2
        if x + 1 < n_x:
            for c in copies(x + 1, 1 - slot):
                c.start()
        for c in copies(x, slot):
            c.wait()
        lhs = jnp.concatenate([tiles[slot, k] for k in range(n_k)], axis=1)
        rhs = blks[slot].reshape(n_k * blks.shape[-2], blks.shape[-1])
        out_ref[x] = jnp.dot(lhs, rhs, preferred_element_type=jnp.float32).astype(out_ref.dtype)


def ladder(places, head, tail, blocks):
    n_nar, n_x, per, t, s = blocks.shape
    n_k = n_nar * per
    rows = head.shape[1] + tail.shape[1]
    return pl.pallas_call(
        functools.partial(ladder_kernel, n_x, n_k, per),
        out_shape=jax.ShapeDtypeStruct((n_x, rows, s), jnp.bfloat16),
        in_specs=[
            pl.BlockSpec(memory_space=pltpu.SMEM),
            pl.BlockSpec(memory_space=pl.ANY),
            pl.BlockSpec(memory_space=pl.ANY),
            pl.BlockSpec(memory_space=pl.ANY),
        ],
        out_specs=pl.BlockSpec(memory_space=pltpu.VMEM),
        scratch_shapes=[
            pltpu.VMEM((2, n_k, rows, t), head.dtype),
            pltpu.VMEM((2, n_nar, per, t, s), blocks.dtype),
            pltpu.SemaphoreType.DMA((2, 3, n_k)),
        ],
        cost_estimate=pl.CostEstimate(
            flops=2 * n_x * n_k * rows * t * s,
            transcendentals=0,
            bytes_accessed=2 * (2 * blocks.size + n_x * rows * s),
        ),
    )(places, head, tail, blocks)


def pick_kernel(n_out, cut, sel_ref, amp_ref, head_ref, tail_ref):
    def body(j, carry):
        tile = amp_ref[sel_ref[j]]
        head_ref[j] = tile[:cut]
        tail_ref[j] = tile[cut:]
        return carry

    lax.fori_loop(0, n_out, body, 0)


def pick_outgoing(amplitudes, selection, cut):
    n_out, (rows, t) = selection.shape[0], amplitudes.shape[1:]
    return pl.pallas_call(
        functools.partial(pick_kernel, n_out, cut),
        out_shape=(
            jax.ShapeDtypeStruct((n_out, cut, t), amplitudes.dtype),
            jax.ShapeDtypeStruct((n_out, rows - cut, t), amplitudes.dtype),
        ),
        in_specs=[pl.BlockSpec(memory_space=pltpu.SMEM), pl.BlockSpec(memory_space=pltpu.VMEM)],
        out_specs=(pl.BlockSpec(memory_space=pltpu.VMEM), pl.BlockSpec(memory_space=pltpu.VMEM)),
        cost_estimate=pl.CostEstimate(flops=0, transcendentals=0, bytes_accessed=4 * n_out * amplitudes[0].size),
    )(selection, amplitudes)


def ladder_kernel(n_x, n_k, per, places_ref, head_hbm, tail_hbm, blk_hbm, out_ref, tiles, blks, sems):
    def copies(x, slot):
        cut = head_hbm.shape[1]
        picked = []
        for k in range(n_k):
            p = places_ref[k // per, x, k % per]
            dst = tiles.at[slot, k]
            picked.append(pltpu.make_async_copy(head_hbm.at[p], dst.at[pl.ds(0, cut)], sems.at[slot, 0, k]))
            picked.append(
                pltpu.make_async_copy(tail_hbm.at[p], dst.at[pl.ds(cut, dst.shape[0] - cut)], sems.at[slot, 1, k])
            )
        return picked + [pltpu.make_async_copy(blk_hbm.at[:, x], blks.at[slot], sems.at[slot, 2, 0])]

    for c in copies(0, 0):
        c.start()
    for x in range(n_x):
        slot = x % 2
        if x + 1 < n_x:
            for c in copies(x + 1, 1 - slot):
                c.start()
        for c in copies(x, slot):
            c.wait()
        lhs = jnp.concatenate([tiles[slot, k] for k in range(n_k)], axis=1)
        rhs = blks[slot].reshape(n_k * blks.shape[-2], blks.shape[-1])
        out_ref[x] = jnp.dot(lhs, rhs, preferred_element_type=jnp.float32).astype(out_ref.dtype)


def ladder(places, head, tail, blocks):
    n_nar, n_x, per, t, s = blocks.shape
    n_k = n_nar * per
    rows = head.shape[1] + tail.shape[1]
    return pl.pallas_call(
        functools.partial(ladder_kernel, n_x, n_k, per),
        out_shape=jax.ShapeDtypeStruct((n_x, rows, s), jnp.bfloat16),
        in_specs=[
            pl.BlockSpec(memory_space=pltpu.SMEM),
            pl.BlockSpec(memory_space=pl.ANY),
            pl.BlockSpec(memory_space=pl.ANY),
            pl.BlockSpec(memory_space=pl.ANY),
        ],
        out_specs=pl.BlockSpec(memory_space=pltpu.VMEM),
        scratch_shapes=[
            pltpu.VMEM((2, n_k, rows, t), head.dtype),
            pltpu.VMEM((2, n_nar, per, t, s), blocks.dtype),
            pltpu.SemaphoreType.DMA((2, 3, n_k)),
        ],
        cost_estimate=pl.CostEstimate(
            flops=2 * n_x * n_k * rows * t * s,
            transcendentals=0,
            bytes_accessed=2 * (2 * blocks.size + n_x * rows * s),
        ),
    )(places, head, tail, blocks)


def pick_kernel(n_out, cut, sel_ref, amp_ref, head_hbm, tail_hbm, sems):
    copies = []
    for j in range(n_out):
        src = amp_ref.at[sel_ref[j]]
        copies.append(pltpu.make_async_copy(src.at[pl.ds(0, cut)], head_hbm.at[j], sems.at[0, j]))
        copies.append(pltpu.make_async_copy(src.at[pl.ds(cut, src.shape[0] - cut)], tail_hbm.at[j], sems.at[1, j]))
    for c in copies:
        c.start()
    for c in copies:
        c.wait()


def pick_outgoing(amplitudes, selection, cut):
    n_out, (rows, t) = selection.shape[0], amplitudes.shape[1:]
    return pl.pallas_call(
        functools.partial(pick_kernel, n_out, cut),
        out_shape=(
            jax.ShapeDtypeStruct((n_out, cut, t), amplitudes.dtype),
            jax.ShapeDtypeStruct((n_out, rows - cut, t), amplitudes.dtype),
        ),
        in_specs=[pl.BlockSpec(memory_space=pltpu.SMEM), pl.BlockSpec(memory_space=pltpu.VMEM)],
        out_specs=(pl.BlockSpec(memory_space=pl.ANY), pl.BlockSpec(memory_space=pl.ANY)),
        scratch_shapes=[pltpu.SemaphoreType.DMA((2, n_out))],
        cost_estimate=pl.CostEstimate(flops=0, transcendentals=0, bytes_accessed=4 * n_out * amplitudes[0].size),
    )(selection, amplitudes)


def on_device(n_nar, amplitudes, send_list, tile_positions, integrals):
    head, tail = pick_outgoing(amplitudes, send_list[0], CUT)
    head = lax.all_to_all(head, "wide", split_axis=0, concat_axis=0, tiled=True)
    tail = lax.all_to_all(tail, "wide", split_axis=0, concat_axis=0, tiled=True)
    lanes = jnp.zeros((tile_positions.shape[0], 128), tile_positions.dtype)
    lanes = lax.dynamic_update_slice(lanes, tile_positions, (0, 0))
    blocks, places = gather_integrals(integrals, lanes, n_nar)
    return ladder(places, head, tail, blocks)


def solution(mesh):
    placed = (
        P("wide", "narrow", None),
        P("wide", None),
        P("wide", "narrow"),
        P("wide", "narrow", None, None),
    )
    return jax.shard_map(
        functools.partial(on_device, mesh.shape["narrow"]),
        mesh=mesh,
        in_specs=placed,
        out_specs=P("wide", "narrow", None),
        check_vma=False,
    )
```

```python
import functools

import jax
import jax.numpy as jnp
from jax import lax
from jax.experimental import pallas as pl
from jax.experimental.pallas import tpu as pltpu
from jax.sharding import PartitionSpec as P

MESH = pl.DeviceIdType.MESH
CUT = 48


def gather_kernel(n_nar, src_ref, pos_ref, dst_ref, pos_dst, send_sem, recv_sem, local_sem):
    me = lax.axis_index("narrow")
    w = lax.axis_index("wide")

    barrier = pltpu.get_barrier_semaphore()
    for i in range(1, n_nar):
        peer = lax.rem(me + i, n_nar)
        pl.semaphore_signal(barrier, 1, device_id=(w, peer), device_id_type=MESH)
    pl.semaphore_wait(barrier, n_nar - 1)

    locals_ = [
        pltpu.make_async_copy(src_ref, dst_ref.at[me], local_sem.at[0]),
        pltpu.make_async_copy(pos_ref, pos_dst.at[me], local_sem.at[1]),
    ]
    for c in locals_:
        c.start()

    def remote(peer, slot):
        return [
            pltpu.make_async_remote_copy(
                src_ref=s,
                dst_ref=d.at[slot],
                send_sem=send_sem.at[part, peer],
                recv_sem=recv_sem.at[part, slot],
                device_id=(w, peer),
                device_id_type=MESH,
            )
            for part, (s, d) in enumerate(((src_ref, dst_ref), (pos_ref, pos_dst)))
        ]

    for i in range(1, n_nar):
        for c in remote(lax.rem(me + i, n_nar), me):
            c.start()
    for i in range(1, n_nar):
        for c in remote(lax.rem(me + i, n_nar), me):
            c.wait_send()
        owner = lax.rem(me + n_nar - i, n_nar)
        for c in remote(owner, owner):
            c.wait_recv()
    for c in locals_:
        c.wait()


def gather_integrals(integrals, positions, n_nar):
    return pl.pallas_call(
        functools.partial(gather_kernel, n_nar),
        out_shape=(
            jax.ShapeDtypeStruct((n_nar,) + integrals.shape, integrals.dtype),
            jax.ShapeDtypeStruct((n_nar,) + positions.shape, positions.dtype),
        ),
        in_specs=[pl.BlockSpec(memory_space=pl.ANY), pl.BlockSpec(memory_space=pl.ANY)],
        out_specs=(pl.BlockSpec(memory_space=pl.ANY), pl.BlockSpec(memory_space=pl.ANY)),
        scratch_shapes=[
            pltpu.SemaphoreType.DMA((2, n_nar)),
            pltpu.SemaphoreType.DMA((2, n_nar)),
            pltpu.SemaphoreType.DMA((2,)),
        ],
        compiler_params=pltpu.CompilerParams(collective_id=0, has_side_effects=True),
        cost_estimate=pl.CostEstimate(
            flops=0, transcendentals=0, bytes_accessed=2 * n_nar * integrals.size * 2
        ),
    )(integrals, positions)


def ladder_kernel(n_x, n_k, per, places_ref, recv_hbm, blk_hbm, out_ref, tiles, blks, sems):
    def copies(x, slot):
        picked = [
            pltpu.make_async_copy(
                recv_hbm.at[places_ref[k // per, x, k % per]], tiles.at[slot, k], sems.at[slot, k]
            )
            for k in range(n_k)
        ]
        return picked + [pltpu.make_async_copy(blk_hbm.at[:, x], blks.at[slot], sems.at[slot, n_k])]

    for c in copies(0, 0):
        c.start()
    for x in range(n_x):
        slot = x % 2
        if x + 1 < n_x:
            for c in copies(x + 1, 1 - slot):
                c.start()
        for c in copies(x, slot):
            c.wait()
        lhs = jnp.concatenate([tiles[slot, k] for k in range(n_k)], axis=1)
        rhs = blks[slot].reshape(n_k * blks.shape[-2], blks.shape[-1])
        out_ref[x] = jnp.dot(lhs, rhs, preferred_element_type=jnp.float32).astype(out_ref.dtype)


def ladder(places, received, blocks):
    n_nar, n_x, per, t, s = blocks.shape
    n_k = n_nar * per
    rows = received.shape[1]
    return pl.pallas_call(
        functools.partial(ladder_kernel, n_x, n_k, per),
        out_shape=jax.ShapeDtypeStruct((n_x, rows, s), jnp.bfloat16),
        in_specs=[
            pl.BlockSpec(memory_space=pltpu.SMEM),
            pl.BlockSpec(memory_space=pl.ANY),
            pl.BlockSpec(memory_space=pl.ANY),
        ],
        out_specs=pl.BlockSpec(memory_space=pltpu.VMEM),
        scratch_shapes=[
            pltpu.VMEM((2, n_k, rows, t), received.dtype),
            pltpu.VMEM((2, n_nar, per, t, s), blocks.dtype),
            pltpu.SemaphoreType.DMA((2, n_k + 1)),
        ],
        cost_estimate=pl.CostEstimate(
            flops=2 * n_x * n_k * rows * t * s,
            transcendentals=0,
            bytes_accessed=2 * (2 * blocks.size + n_x * rows * s),
        ),
    )(places, received, blocks)


def pick_kernel(n_out, cut, sel_ref, amp_ref, head_hbm, tail_hbm, sems):
    copies = []
    for j in range(n_out):
        src = amp_ref.at[sel_ref[j]]
        copies.append(pltpu.make_async_copy(src.at[pl.ds(0, cut)], head_hbm.at[j], sems.at[0, j]))
        copies.append(pltpu.make_async_copy(src.at[pl.ds(cut, src.shape[0] - cut)], tail_hbm.at[j], sems.at[1, j]))
    for c in copies:
        c.start()
    for c in copies:
        c.wait()


def pick_outgoing(amplitudes, selection, cut):
    n_out, (rows, t) = selection.shape[0], amplitudes.shape[1:]
    return pl.pallas_call(
        functools.partial(pick_kernel, n_out, cut),
        out_shape=(
            jax.ShapeDtypeStruct((n_out, cut, t), amplitudes.dtype),
            jax.ShapeDtypeStruct((n_out, rows - cut, t), amplitudes.dtype),
        ),
        in_specs=[pl.BlockSpec(memory_space=pltpu.SMEM), pl.BlockSpec(memory_space=pltpu.VMEM)],
        out_specs=(pl.BlockSpec(memory_space=pl.ANY), pl.BlockSpec(memory_space=pl.ANY)),
        scratch_shapes=[pltpu.SemaphoreType.DMA((2, n_out))],
        cost_estimate=pl.CostEstimate(flops=0, transcendentals=0, bytes_accessed=4 * n_out * amplitudes[0].size),
    )(selection, amplitudes)


def on_device(n_nar, amplitudes, send_list, tile_positions, integrals):
    head, tail = pick_outgoing(amplitudes, send_list[0], CUT)
    head = lax.all_to_all(head, "wide", split_axis=0, concat_axis=0, tiled=True)
    tail = lax.all_to_all(tail, "wide", split_axis=0, concat_axis=0, tiled=True)
    lanes = jnp.zeros((tile_positions.shape[0], 128), tile_positions.dtype)
    lanes = lax.dynamic_update_slice(lanes, tile_positions, (0, 0))
    blocks, places = gather_integrals(integrals, lanes, n_nar)
    rows = [ladder(places, part, blocks) for part in (head, tail)]
    return jnp.concatenate(rows, axis=1)


def solution(mesh):
    placed = (
        P("wide", "narrow", None),
        P("wide", None),
        P("wide", "narrow"),
        P("wide", "narrow", None, None),
    )
    return jax.shard_map(
        functools.partial(on_device, mesh.shape["narrow"]),
        mesh=mesh,
        in_specs=placed,
        out_specs=P("wide", "narrow", None),
        check_vma=False,
    )
```

```python
import functools

import jax
import jax.numpy as jnp
from jax import lax
from jax.experimental import pallas as pl
from jax.experimental.pallas import tpu as pltpu
from jax.sharding import PartitionSpec as P

MESH = pl.DeviceIdType.MESH
CUT = 48


def gather_kernel(n_nar, src_ref, pos_ref, dst_ref, pos_dst, send_sem, recv_sem, local_sem):
    me = lax.axis_index("narrow")
    w = lax.axis_index("wide")

    barrier = pltpu.get_barrier_semaphore()
    for i in range(1, n_nar):
        peer = lax.rem(me + i, n_nar)
        pl.semaphore_signal(barrier, 1, device_id=(w, peer), device_id_type=MESH)
    pl.semaphore_wait(barrier, n_nar - 1)

    locals_ = [
        pltpu.make_async_copy(src_ref, dst_ref.at[me], local_sem.at[0]),
        pltpu.make_async_copy(pos_ref, pos_dst.at[me], local_sem.at[1]),
    ]
    for c in locals_:
        c.start()

    def remote(peer, slot):
        return [
            pltpu.make_async_remote_copy(
                src_ref=s,
                dst_ref=d.at[slot],
                send_sem=send_sem.at[part, peer],
                recv_sem=recv_sem.at[part, slot],
                device_id=(w, peer),
                device_id_type=MESH,
            )
            for part, (s, d) in enumerate(((src_ref, dst_ref), (pos_ref, pos_dst)))
        ]

    for i in range(1, n_nar):
        for c in remote(lax.rem(me + i, n_nar), me):
            c.start()
    for i in range(1, n_nar):
        for c in remote(lax.rem(me + i, n_nar), me):
            c.wait_send()
        owner = lax.rem(me + n_nar - i, n_nar)
        for c in remote(owner, owner):
            c.wait_recv()
    for c in locals_:
        c.wait()


def gather_integrals(integrals, positions, n_nar):
    return pl.pallas_call(
        functools.partial(gather_kernel, n_nar),
        out_shape=(
            jax.ShapeDtypeStruct((n_nar,) + integrals.shape, integrals.dtype),
            jax.ShapeDtypeStruct((n_nar,) + positions.shape, positions.dtype),
        ),
        in_specs=[pl.BlockSpec(memory_space=pl.ANY), pl.BlockSpec(memory_space=pl.ANY)],
        out_specs=(pl.BlockSpec(memory_space=pl.ANY), pl.BlockSpec(memory_space=pl.ANY)),
        scratch_shapes=[
            pltpu.SemaphoreType.DMA((2, n_nar)),
            pltpu.SemaphoreType.DMA((2, n_nar)),
            pltpu.SemaphoreType.DMA((2,)),
        ],
        compiler_params=pltpu.CompilerParams(collective_id=0, has_side_effects=True),
        cost_estimate=pl.CostEstimate(
            flops=0, transcendentals=0, bytes_accessed=2 * n_nar * integrals.size * 2
        ),
    )(integrals, positions)


def ladder_kernel(n_x, n_k, per, places_ref, head_hbm, tail_hbm, blk_hbm, out_ref, tiles, blks, sems):
    def copies(x, slot):
        cut = head_hbm.shape[1]
        picked = []
        for k in range(n_k):
            p = places_ref[k // per, x, k % per]
            dst = tiles.at[slot, k]
            picked.append(pltpu.make_async_copy(head_hbm.at[p], dst.at[pl.ds(0, cut)], sems.at[slot, 0, k]))
            picked.append(
                pltpu.make_async_copy(tail_hbm.at[p], dst.at[pl.ds(cut, dst.shape[0] - cut)], sems.at[slot, 1, k])
            )
        return picked + [pltpu.make_async_copy(blk_hbm.at[:, x], blks.at[slot], sems.at[slot, 2, 0])]

    for c in copies(0, 0):
        c.start()
    for x in range(n_x):
        slot = x % 2
        if x + 1 < n_x:
            for c in copies(x + 1, 1 - slot):
                c.start()
        for c in copies(x, slot):
            c.wait()
        lhs = jnp.concatenate([tiles[slot, k] for k in range(n_k)], axis=1)
        rhs = blks[slot].reshape(n_k * blks.shape[-2], blks.shape[-1])
        out_ref[x] = jnp.dot(lhs, rhs, preferred_element_type=jnp.float32).astype(out_ref.dtype)


def ladder(places, head, tail, blocks):
    n_nar, n_x, per, t, s = blocks.shape
    n_k = n_nar * per
    rows = head.shape[1] + tail.shape[1]
    return pl.pallas_call(
        functools.partial(ladder_kernel, n_x, n_k, per),
        out_shape=jax.ShapeDtypeStruct((n_x, rows, s), jnp.bfloat16),
        in_specs=[
            pl.BlockSpec(memory_space=pltpu.SMEM),
            pl.BlockSpec(memory_space=pl.ANY),
            pl.BlockSpec(memory_space=pl.ANY),
            pl.BlockSpec(memory_space=pl.ANY),
        ],
        out_specs=pl.BlockSpec(memory_space=pltpu.VMEM),
        scratch_shapes=[
            pltpu.VMEM((2, n_k, rows, t), head.dtype),
            pltpu.VMEM((2, n_nar, per, t, s), blocks.dtype),
            pltpu.SemaphoreType.DMA((2, 3, n_k)),
        ],
        cost_estimate=pl.CostEstimate(
            flops=2 * n_x * n_k * rows * t * s,
            transcendentals=0,
            bytes_accessed=2 * (2 * blocks.size + n_x * rows * s),
        ),
    )(places, head, tail, blocks)


def pick_kernel(n_out, cut, sel_ref, amp_ref, head_ref, tail_ref):
    def body(j, carry):
        tile = amp_ref[sel_ref[j]]
        head_ref[j] = tile[:cut]
        tail_ref[j] = tile[cut:]
        return carry

    lax.fori_loop(0, n_out, body, 0)


def pick_outgoing(amplitudes, selection, cut):
    n_out, (rows, t) = selection.shape[0], amplitudes.shape[1:]
    return pl.pallas_call(
        functools.partial(pick_kernel, n_out, cut),
        out_shape=(
            jax.ShapeDtypeStruct((n_out, cut, t), amplitudes.dtype),
            jax.ShapeDtypeStruct((n_out, rows - cut, t), amplitudes.dtype),
        ),
        in_specs=[pl.BlockSpec(memory_space=pltpu.SMEM), pl.BlockSpec(memory_space=pltpu.VMEM)],
        out_specs=(pl.BlockSpec(memory_space=pltpu.VMEM), pl.BlockSpec(memory_space=pltpu.VMEM)),
        cost_estimate=pl.CostEstimate(flops=0, transcendentals=0, bytes_accessed=4 * n_out * amplitudes[0].size),
    )(selection, amplitudes)


def on_device(n_nar, amplitudes, send_list, tile_positions, integrals):
    head, tail = pick_outgoing(amplitudes, send_list[0], CUT)
    head = lax.all_to_all(head, "wide", split_axis=0, concat_axis=0, tiled=True)
    tail = lax.all_to_all(tail, "wide", split_axis=0, concat_axis=0, tiled=True)
    lanes = jnp.zeros((tile_positions.shape[0], 128), tile_positions.dtype)
    lanes = lax.dynamic_update_slice(lanes, tile_positions, (0, 0))
    blocks, places = gather_integrals(integrals, lanes, n_nar)
    return ladder(places, head, tail, blocks)


def solution(mesh):
    placed = (
        P("wide", "narrow", None),
        P("wide", None),
        P("wide", "narrow"),
        P("wide", "narrow", None, None),
    )
    return jax.shard_map(
        functools.partial(on_device, mesh.shape["narrow"]),
        mesh=mesh,
        in_specs=placed,
        out_specs=P("wide", "narrow", None),
        check_vma=False,
    )
```

```python
import functools

import jax
import jax.numpy as jnp
from jax import lax
from jax.experimental import pallas as pl
from jax.experimental.pallas import tpu as pltpu
from jax.sharding import PartitionSpec as P

MESH = pl.DeviceIdType.MESH
CUT = 48


def gather_kernel(n_nar, src_ref, pos_ref, dst_ref, pos_dst, send_sem, recv_sem, local_sem):
    me = lax.axis_index("narrow")
    w = lax.axis_index("wide")

    barrier = pltpu.get_barrier_semaphore()
    for i in range(1, n_nar):
        peer = lax.rem(me + i, n_nar)
        pl.semaphore_signal(barrier, 1, device_id=(w, peer), device_id_type=MESH)
    pl.semaphore_wait(barrier, n_nar - 1)

    locals_ = [
        pltpu.make_async_copy(src_ref, dst_ref.at[me], local_sem.at[0]),
        pltpu.make_async_copy(pos_ref, pos_dst.at[me], local_sem.at[1]),
    ]
    for c in locals_:
        c.start()

    def remote(peer, slot):
        return [
            pltpu.make_async_remote_copy(
                src_ref=s,
                dst_ref=d.at[slot],
                send_sem=send_sem.at[part, peer],
                recv_sem=recv_sem.at[part, slot],
                device_id=(w, peer),
                device_id_type=MESH,
            )
            for part, (s, d) in enumerate(((src_ref, dst_ref), (pos_ref, pos_dst)))
        ]

    for i in range(1, n_nar):
        for c in remote(lax.rem(me + i, n_nar), me):
            c.start()
    for i in range(1, n_nar):
        for c in remote(lax.rem(me + i, n_nar), me):
            c.wait_send()
        owner = lax.rem(me + n_nar - i, n_nar)
        for c in remote(owner, owner):
            c.wait_recv()
    for c in locals_:
        c.wait()


def gather_integrals(integrals, positions, n_nar):
    return pl.pallas_call(
        functools.partial(gather_kernel, n_nar),
        out_shape=(
            jax.ShapeDtypeStruct((n_nar,) + integrals.shape, integrals.dtype),
            jax.ShapeDtypeStruct((n_nar,) + positions.shape, positions.dtype),
        ),
        in_specs=[pl.BlockSpec(memory_space=pl.ANY), pl.BlockSpec(memory_space=pl.ANY)],
        out_specs=(pl.BlockSpec(memory_space=pl.ANY), pl.BlockSpec(memory_space=pl.ANY)),
        scratch_shapes=[
            pltpu.SemaphoreType.DMA((2, n_nar)),
            pltpu.SemaphoreType.DMA((2, n_nar)),
            pltpu.SemaphoreType.DMA((2,)),
        ],
        compiler_params=pltpu.CompilerParams(collective_id=0, has_side_effects=True),
        cost_estimate=pl.CostEstimate(
            flops=0, transcendentals=0, bytes_accessed=2 * n_nar * integrals.size * 2
        ),
    )(integrals, positions)


def ladder_kernel(n_x, n_k, per, places_ref, head_hbm, tail_hbm, blk_hbm, out_ref, tiles, blks, sems):
    cut = head_hbm.shape[1]

    def copies(pair, slot):
        out = []
        for sub in range(2):
            x = 2 * pair + sub
            for k in range(n_k):
                p = places_ref[k // per, x, k % per]
                dst = tiles.at[slot, sub, k]
                out.append(pltpu.make_async_copy(head_hbm.at[p], dst.at[pl.ds(0, cut)], sems.at[slot, sub, 0, k]))
                out.append(
                    pltpu.make_async_copy(
                        tail_hbm.at[p], dst.at[pl.ds(cut, dst.shape[0] - cut)], sems.at[slot, sub, 1, k]
                    )
                )
            out.append(pltpu.make_async_copy(blk_hbm.at[:, x], blks.at[slot, sub], sems.at[slot, sub, 2, 0]))
        return out

    n_pairs = n_x // 2
    for c in copies(0, 0):
        c.start()
    for pair in range(n_pairs):
        slot = pair % 2
        if pair + 1 < n_pairs:
            for c in copies(pair + 1, 1 - slot):
                c.start()
        for c in copies(pair, slot):
            c.wait()
        lhs = jnp.concatenate(
            [jnp.concatenate([tiles[slot, sub, k] for k in range(n_k)], axis=1) for sub in range(2)], axis=0
        )
        rhs = jnp.concatenate(
            [blks[slot, sub].reshape(n_k * blks.shape[-2], blks.shape[-1]) for sub in range(2)], axis=1
        )
        res = jnp.dot(lhs, rhs, preferred_element_type=jnp.float32)
        rows, cols = tiles.shape[-2], blks.shape[-1]
        out_ref[2 * pair] = res[:rows, :cols].astype(out_ref.dtype)
        out_ref[2 * pair + 1] = res[rows:, cols:].astype(out_ref.dtype)


def ladder(places, head, tail, blocks):
    n_nar, n_x, per, t, s = blocks.shape
    n_k = n_nar * per
    rows = head.shape[1] + tail.shape[1]
    return pl.pallas_call(
        functools.partial(ladder_kernel, n_x, n_k, per),
        out_shape=jax.ShapeDtypeStruct((n_x, rows, s), jnp.bfloat16),
        in_specs=[
            pl.BlockSpec(memory_space=pltpu.SMEM),
            pl.BlockSpec(memory_space=pl.ANY),
            pl.BlockSpec(memory_space=pl.ANY),
            pl.BlockSpec(memory_space=pl.ANY),
        ],
        out_specs=pl.BlockSpec(memory_space=pltpu.VMEM),
        scratch_shapes=[
            pltpu.VMEM((2, 2, n_k, rows, t), head.dtype),
            pltpu.VMEM((2, 2, n_nar, per, t, s), blocks.dtype),
            pltpu.SemaphoreType.DMA((2, 2, 3, n_k)),
        ],
        cost_estimate=pl.CostEstimate(
            flops=2 * n_x * n_k * rows * t * s,
            transcendentals=0,
            bytes_accessed=2 * (2 * blocks.size + n_x * rows * s),
        ),
    )(places, head, tail, blocks)


def pick_kernel(n_out, cut, sel_ref, amp_ref, head_ref, tail_ref):
    def body(j, carry):
        tile = amp_ref[sel_ref[j]]
        head_ref[j] = tile[:cut]
        tail_ref[j] = tile[cut:]
        return carry

    lax.fori_loop(0, n_out, body, 0)


def pick_outgoing(amplitudes, selection, cut):
    n_out, (rows, t) = selection.shape[0], amplitudes.shape[1:]
    return pl.pallas_call(
        functools.partial(pick_kernel, n_out, cut),
        out_shape=(
            jax.ShapeDtypeStruct((n_out, cut, t), amplitudes.dtype),
            jax.ShapeDtypeStruct((n_out, rows - cut, t), amplitudes.dtype),
        ),
        in_specs=[pl.BlockSpec(memory_space=pltpu.SMEM), pl.BlockSpec(memory_space=pltpu.VMEM)],
        out_specs=(pl.BlockSpec(memory_space=pltpu.VMEM), pl.BlockSpec(memory_space=pltpu.VMEM)),
        cost_estimate=pl.CostEstimate(flops=0, transcendentals=0, bytes_accessed=4 * n_out * amplitudes[0].size),
    )(selection, amplitudes)


def on_device(n_nar, amplitudes, send_list, tile_positions, integrals):
    head, tail = pick_outgoing(amplitudes, send_list[0], CUT)
    head = lax.all_to_all(head, "wide", split_axis=0, concat_axis=0, tiled=True)
    tail = lax.all_to_all(tail, "wide", split_axis=0, concat_axis=0, tiled=True)
    lanes = jnp.zeros((tile_positions.shape[0], 128), tile_positions.dtype)
    lanes = lax.dynamic_update_slice(lanes, tile_positions, (0, 0))
    blocks, places = gather_integrals(integrals, lanes, n_nar)
    return ladder(places, head, tail, blocks)


def solution(mesh):
    placed = (
        P("wide", "narrow", None),
        P("wide", None),
        P("wide", "narrow"),
        P("wide", "narrow", None, None),
    )
    return jax.shard_map(
        functools.partial(on_device, mesh.shape["narrow"]),
        mesh=mesh,
        in_specs=placed,
        out_specs=P("wide", "narrow", None),
        check_vma=False,
    )
```

```python
import functools

import jax
import jax.numpy as jnp
from jax import lax
from jax.experimental import pallas as pl
from jax.experimental.pallas import tpu as pltpu
from jax.sharding import PartitionSpec as P

MESH = pl.DeviceIdType.MESH
CUT = 48


def gather_kernel(n_nar, src_ref, pos_ref, dst_ref, pos_dst, send_sem, recv_sem, local_sem):
    me = lax.axis_index("narrow")
    w = lax.axis_index("wide")

    barrier = pltpu.get_barrier_semaphore()
    for i in range(1, n_nar):
        peer = lax.rem(me + i, n_nar)
        pl.semaphore_signal(barrier, 1, device_id=(w, peer), device_id_type=MESH)
    pl.semaphore_wait(barrier, n_nar - 1)

    locals_ = [
        pltpu.make_async_copy(src_ref, dst_ref.at[me], local_sem.at[0]),
        pltpu.make_async_copy(pos_ref, pos_dst.at[me], local_sem.at[1]),
    ]
    for c in locals_:
        c.start()

    def remote(peer, slot):
        return [
            pltpu.make_async_remote_copy(
                src_ref=s,
                dst_ref=d.at[slot],
                send_sem=send_sem.at[part, peer],
                recv_sem=recv_sem.at[part, slot],
                device_id=(w, peer),
                device_id_type=MESH,
            )
            for part, (s, d) in enumerate(((src_ref, dst_ref), (pos_ref, pos_dst)))
        ]

    for i in range(1, n_nar):
        for c in remote(lax.rem(me + i, n_nar), me):
            c.start()
    for i in range(1, n_nar):
        for c in remote(lax.rem(me + i, n_nar), me):
            c.wait_send()
        owner = lax.rem(me + n_nar - i, n_nar)
        for c in remote(owner, owner):
            c.wait_recv()
    for c in locals_:
        c.wait()


def gather_integrals(integrals, positions, n_nar):
    return pl.pallas_call(
        functools.partial(gather_kernel, n_nar),
        out_shape=(
            jax.ShapeDtypeStruct((n_nar,) + integrals.shape, integrals.dtype),
            jax.ShapeDtypeStruct((n_nar,) + positions.shape, positions.dtype),
        ),
        in_specs=[pl.BlockSpec(memory_space=pl.ANY), pl.BlockSpec(memory_space=pl.ANY)],
        out_specs=(pl.BlockSpec(memory_space=pl.ANY), pl.BlockSpec(memory_space=pl.ANY)),
        scratch_shapes=[
            pltpu.SemaphoreType.DMA((2, n_nar)),
            pltpu.SemaphoreType.DMA((2, n_nar)),
            pltpu.SemaphoreType.DMA((2,)),
        ],
        compiler_params=pltpu.CompilerParams(collective_id=0, has_side_effects=True),
        cost_estimate=pl.CostEstimate(
            flops=0, transcendentals=0, bytes_accessed=2 * n_nar * integrals.size * 2
        ),
    )(integrals, positions)


def ladder_kernel(n_x, n_k, per, places_ref, head_hbm, tail_hbm, blk_hbm, out_ref, head_v, tail_v, blks, sems):
    whole = [
        pltpu.make_async_copy(head_hbm, head_v, sems.at[0]),
        pltpu.make_async_copy(tail_hbm, tail_v, sems.at[1]),
    ]

    def blk_copy(x, slot):
        return pltpu.make_async_copy(blk_hbm.at[:, x], blks.at[slot], sems.at[2 + slot])

    for c in whole:
        c.start()
    blk_copy(0, 0).start()
    for c in whole:
        c.wait()
    for x in range(n_x):
        slot = x % 2
        if x + 1 < n_x:
            blk_copy(x + 1, 1 - slot).start()
        blk_copy(x, slot).wait()
        picked = []
        for k in range(n_k):
            p = places_ref[k // per, x, k % per]
            picked.append(jnp.concatenate([head_v[p], tail_v[p]], axis=0))
        lhs = jnp.concatenate(picked, axis=1)
        rhs = blks[slot].reshape(n_k * blks.shape[-2], blks.shape[-1])
        out_ref[x] = jnp.dot(lhs, rhs, preferred_element_type=jnp.float32).astype(out_ref.dtype)


def ladder(places, head, tail, blocks):
    n_nar, n_x, per, t, s = blocks.shape
    n_k = n_nar * per
    rows = head.shape[1] + tail.shape[1]
    return pl.pallas_call(
        functools.partial(ladder_kernel, n_x, n_k, per),
        out_shape=jax.ShapeDtypeStruct((n_x, rows, s), jnp.bfloat16),
        in_specs=[
            pl.BlockSpec(memory_space=pltpu.SMEM),
            pl.BlockSpec(memory_space=pl.ANY),
            pl.BlockSpec(memory_space=pl.ANY),
            pl.BlockSpec(memory_space=pl.ANY),
        ],
        out_specs=pl.BlockSpec(memory_space=pltpu.VMEM),
        scratch_shapes=[
            pltpu.VMEM(head.shape, head.dtype),
            pltpu.VMEM(tail.shape, tail.dtype),
            pltpu.VMEM((2, n_nar, per, t, s), blocks.dtype),
            pltpu.SemaphoreType.DMA((4,)),
        ],
        cost_estimate=pl.CostEstimate(
            flops=2 * n_x * n_k * rows * t * s,
            transcendentals=0,
            bytes_accessed=2 * (2 * blocks.size + n_x * rows * s),
        ),
    )(places, head, tail, blocks)


def pick_kernel(n_out, cut, sel_ref, amp_ref, head_ref, tail_ref):
    def body(j, carry):
        tile = amp_ref[sel_ref[j]]
        head_ref[j] = tile[:cut]
        tail_ref[j] = tile[cut:]
        return carry

    lax.fori_loop(0, n_out, body, 0)


def pick_outgoing(amplitudes, selection, cut):
    n_out, (rows, t) = selection.shape[0], amplitudes.shape[1:]
    return pl.pallas_call(
        functools.partial(pick_kernel, n_out, cut),
        out_shape=(
            jax.ShapeDtypeStruct((n_out, cut, t), amplitudes.dtype),
            jax.ShapeDtypeStruct((n_out, rows - cut, t), amplitudes.dtype),
        ),
        in_specs=[pl.BlockSpec(memory_space=pltpu.SMEM), pl.BlockSpec(memory_space=pltpu.VMEM)],
        out_specs=(pl.BlockSpec(memory_space=pltpu.VMEM), pl.BlockSpec(memory_space=pltpu.VMEM)),
        cost_estimate=pl.CostEstimate(flops=0, transcendentals=0, bytes_accessed=4 * n_out * amplitudes[0].size),
    )(selection, amplitudes)


def on_device(n_nar, amplitudes, send_list, tile_positions, integrals):
    head, tail = pick_outgoing(amplitudes, send_list[0], CUT)
    head = lax.all_to_all(head, "wide", split_axis=0, concat_axis=0, tiled=True)
    tail = lax.all_to_all(tail, "wide", split_axis=0, concat_axis=0, tiled=True)
    lanes = jnp.zeros((tile_positions.shape[0], 128), tile_positions.dtype)
    lanes = lax.dynamic_update_slice(lanes, tile_positions, (0, 0))
    blocks, places = gather_integrals(integrals, lanes, n_nar)
    return ladder(places, head, tail, blocks)


def solution(mesh):
    placed = (
        P("wide", "narrow", None),
        P("wide", None),
        P("wide", "narrow"),
        P("wide", "narrow", None, None),
    )
    return jax.shard_map(
        functools.partial(on_device, mesh.shape["narrow"]),
        mesh=mesh,
        in_specs=placed,
        out_specs=P("wide", "narrow", None),
        check_vma=False,
    )
```

```python
import functools

import jax
import jax.numpy as jnp
from jax import lax
from jax.experimental import pallas as pl
from jax.experimental.pallas import tpu as pltpu
from jax.sharding import PartitionSpec as P

MESH = pl.DeviceIdType.MESH
CUT = 48


def gather_kernel(n_nar, src_ref, pos_ref, dst_ref, pos_dst, send_sem, recv_sem, local_sem):
    me = lax.axis_index("narrow")
    w = lax.axis_index("wide")

    barrier = pltpu.get_barrier_semaphore()
    for i in range(1, n_nar):
        peer = lax.rem(me + i, n_nar)
        pl.semaphore_signal(barrier, 1, device_id=(w, peer), device_id_type=MESH)
    pl.semaphore_wait(barrier, n_nar - 1)

    locals_ = [
        pltpu.make_async_copy(src_ref, dst_ref.at[me], local_sem.at[0]),
        pltpu.make_async_copy(pos_ref, pos_dst.at[me], local_sem.at[1]),
    ]
    for c in locals_:
        c.start()

    def remote(peer, slot):
        return [
            pltpu.make_async_remote_copy(
                src_ref=s,
                dst_ref=d.at[slot],
                send_sem=send_sem.at[part, peer],
                recv_sem=recv_sem.at[part, slot],
                device_id=(w, peer),
                device_id_type=MESH,
            )
            for part, (s, d) in enumerate(((src_ref, dst_ref), (pos_ref, pos_dst)))
        ]

    for i in range(1, n_nar):
        for c in remote(lax.rem(me + i, n_nar), me):
            c.start()
    for i in range(1, n_nar):
        for c in remote(lax.rem(me + i, n_nar), me):
            c.wait_send()
        owner = lax.rem(me + n_nar - i, n_nar)
        for c in remote(owner, owner):
            c.wait_recv()
    for c in locals_:
        c.wait()


def gather_integrals(integrals, positions, n_nar):
    return pl.pallas_call(
        functools.partial(gather_kernel, n_nar),
        out_shape=(
            jax.ShapeDtypeStruct((n_nar,) + integrals.shape, integrals.dtype),
            jax.ShapeDtypeStruct((n_nar,) + positions.shape, positions.dtype),
        ),
        in_specs=[pl.BlockSpec(memory_space=pl.ANY), pl.BlockSpec(memory_space=pl.ANY)],
        out_specs=(pl.BlockSpec(memory_space=pl.ANY), pl.BlockSpec(memory_space=pl.ANY)),
        scratch_shapes=[
            pltpu.SemaphoreType.DMA((2, n_nar)),
            pltpu.SemaphoreType.DMA((2, n_nar)),
            pltpu.SemaphoreType.DMA((2,)),
        ],
        compiler_params=pltpu.CompilerParams(collective_id=0, has_side_effects=True),
        cost_estimate=pl.CostEstimate(
            flops=0, transcendentals=0, bytes_accessed=2 * n_nar * integrals.size * 2
        ),
    )(integrals, positions)


def ladder_kernel(n_x, n_k, per, places_ref, head_hbm, tail_hbm, blk_hbm, out_ref, head_v, tail_v, blk_v, sems):
    whole = [
        pltpu.make_async_copy(head_hbm, head_v, sems.at[0]),
        pltpu.make_async_copy(tail_hbm, tail_v, sems.at[1]),
        pltpu.make_async_copy(blk_hbm, blk_v, sems.at[2]),
    ]
    for c in whole:
        c.start()
    for c in whole:
        c.wait()
    for x in range(n_x):
        picked = []
        for k in range(n_k):
            p = places_ref[k // per, x, k % per]
            picked.append(jnp.concatenate([head_v[p], tail_v[p]], axis=0))
        lhs = jnp.concatenate(picked, axis=1)
        rhs = blk_v[:, x].reshape(n_k * blk_v.shape[-2], blk_v.shape[-1])
        out_ref[x] = jnp.dot(lhs, rhs, preferred_element_type=jnp.float32).astype(out_ref.dtype)


def ladder(places, head, tail, blocks):
    n_nar, n_x, per, t, s = blocks.shape
    n_k = n_nar * per
    rows = head.shape[1] + tail.shape[1]
    return pl.pallas_call(
        functools.partial(ladder_kernel, n_x, n_k, per),
        out_shape=jax.ShapeDtypeStruct((n_x, rows, s), jnp.bfloat16),
        in_specs=[
            pl.BlockSpec(memory_space=pltpu.SMEM),
            pl.BlockSpec(memory_space=pl.ANY),
            pl.BlockSpec(memory_space=pl.ANY),
            pl.BlockSpec(memory_space=pl.ANY),
        ],
        out_specs=pl.BlockSpec(memory_space=pltpu.VMEM),
        scratch_shapes=[
            pltpu.VMEM(head.shape, head.dtype),
            pltpu.VMEM(tail.shape, tail.dtype),
            pltpu.VMEM(blocks.shape, blocks.dtype),
            pltpu.SemaphoreType.DMA((3,)),
        ],
        cost_estimate=pl.CostEstimate(
            flops=2 * n_x * n_k * rows * t * s,
            transcendentals=0,
            bytes_accessed=2 * (2 * blocks.size + n_x * rows * s),
        ),
    )(places, head, tail, blocks)


def pick_kernel(n_out, cut, sel_ref, amp_ref, head_ref, tail_ref):
    def body(j, carry):
        tile = amp_ref[sel_ref[j]]
        head_ref[j] = tile[:cut]
        tail_ref[j] = tile[cut:]
        return carry

    lax.fori_loop(0, n_out, body, 0)


def pick_outgoing(amplitudes, selection, cut):
    n_out, (rows, t) = selection.shape[0], amplitudes.shape[1:]
    return pl.pallas_call(
        functools.partial(pick_kernel, n_out, cut),
        out_shape=(
            jax.ShapeDtypeStruct((n_out, cut, t), amplitudes.dtype),
            jax.ShapeDtypeStruct((n_out, rows - cut, t), amplitudes.dtype),
        ),
        in_specs=[pl.BlockSpec(memory_space=pltpu.SMEM), pl.BlockSpec(memory_space=pltpu.VMEM)],
        out_specs=(pl.BlockSpec(memory_space=pltpu.VMEM), pl.BlockSpec(memory_space=pltpu.VMEM)),
        cost_estimate=pl.CostEstimate(flops=0, transcendentals=0, bytes_accessed=4 * n_out * amplitudes[0].size),
    )(selection, amplitudes)


def on_device(n_nar, amplitudes, send_list, tile_positions, integrals):
    head, tail = pick_outgoing(amplitudes, send_list[0], CUT)
    head = lax.all_to_all(head, "wide", split_axis=0, concat_axis=0, tiled=True)
    tail = lax.all_to_all(tail, "wide", split_axis=0, concat_axis=0, tiled=True)
    lanes = jnp.zeros((tile_positions.shape[0], 128), tile_positions.dtype)
    lanes = lax.dynamic_update_slice(lanes, tile_positions, (0, 0))
    blocks, places = gather_integrals(integrals, lanes, n_nar)
    return ladder(places, head, tail, blocks)


def solution(mesh):
    placed = (
        P("wide", "narrow", None),
        P("wide", None),
        P("wide", "narrow"),
        P("wide", "narrow", None, None),
    )
    return jax.shard_map(
        functools.partial(on_device, mesh.shape["narrow"]),
        mesh=mesh,
        in_specs=placed,
        out_specs=P("wide", "narrow", None),
        check_vma=False,
    )
```

```python
import functools

import jax
import jax.numpy as jnp
from jax import lax
from jax.experimental import pallas as pl
from jax.experimental.pallas import tpu as pltpu
from jax.sharding import PartitionSpec as P

MESH = pl.DeviceIdType.MESH
CUT = 48


def gather_kernel(n_nar, src_ref, pos_ref, dst_ref, pos_dst, send_sem, recv_sem, local_sem):
    me = lax.axis_index("narrow")
    w = lax.axis_index("wide")

    barrier = pltpu.get_barrier_semaphore()
    for i in range(1, n_nar):
        peer = lax.rem(me + i, n_nar)
        pl.semaphore_signal(barrier, 1, device_id=(w, peer), device_id_type=MESH)
    pl.semaphore_wait(barrier, n_nar - 1)

    locals_ = [
        pltpu.make_async_copy(src_ref, dst_ref.at[me], local_sem.at[0]),
        pltpu.make_async_copy(pos_ref, pos_dst.at[me], local_sem.at[1]),
    ]
    for c in locals_:
        c.start()

    def remote(peer, slot):
        return [
            pltpu.make_async_remote_copy(
                src_ref=s,
                dst_ref=d.at[slot],
                send_sem=send_sem.at[part, peer],
                recv_sem=recv_sem.at[part, slot],
                device_id=(w, peer),
                device_id_type=MESH,
            )
            for part, (s, d) in enumerate(((src_ref, dst_ref), (pos_ref, pos_dst)))
        ]

    for i in range(1, n_nar):
        for c in remote(lax.rem(me + i, n_nar), me):
            c.start()
    for i in range(1, n_nar):
        for c in remote(lax.rem(me + i, n_nar), me):
            c.wait_send()
        owner = lax.rem(me + n_nar - i, n_nar)
        for c in remote(owner, owner):
            c.wait_recv()
    for c in locals_:
        c.wait()


def gather_integrals(integrals, positions, n_nar):
    return pl.pallas_call(
        functools.partial(gather_kernel, n_nar),
        out_shape=(
            jax.ShapeDtypeStruct((n_nar,) + integrals.shape, integrals.dtype),
            jax.ShapeDtypeStruct((n_nar,) + positions.shape, positions.dtype),
        ),
        in_specs=[pl.BlockSpec(memory_space=pl.ANY), pl.BlockSpec(memory_space=pl.ANY)],
        out_specs=(pl.BlockSpec(memory_space=pl.ANY), pl.BlockSpec(memory_space=pl.ANY)),
        scratch_shapes=[
            pltpu.SemaphoreType.DMA((2, n_nar)),
            pltpu.SemaphoreType.DMA((2, n_nar)),
            pltpu.SemaphoreType.DMA((2,)),
        ],
        compiler_params=pltpu.CompilerParams(collective_id=0, has_side_effects=True),
        cost_estimate=pl.CostEstimate(
            flops=0, transcendentals=0, bytes_accessed=2 * n_nar * integrals.size * 2
        ),
    )(integrals, positions)


def ladder_kernel(n_x, n_k, per, places_ref, head_hbm, tail_hbm, blk_hbm, out_ref, head_v, tail_v, blk_v, acc, sems):
    half = blk_v.shape[0] // 2
    parts = (pl.ds(0, half), pl.ds(half, blk_v.shape[0] - half))
    copies = [
        pltpu.make_async_copy(head_hbm, head_v, sems.at[0]),
        pltpu.make_async_copy(tail_hbm, tail_v, sems.at[1]),
    ] + [pltpu.make_async_copy(blk_hbm.at[r], blk_v.at[r], sems.at[2 + i]) for i, r in enumerate(parts)]
    for c in copies:
        c.start()
    for c in copies[:3]:
        c.wait()
    for h, r in enumerate(parts):
        if h == 1:
            copies[3].wait()
        ks = range(h * half * per, (h * half + r.size) * per)
        for x in range(n_x):
            picked = []
            for k in ks:
                p = places_ref[k // per, x, k % per]
                picked.append(jnp.concatenate([head_v[p], tail_v[p]], axis=0))
            lhs = jnp.concatenate(picked, axis=1)
            rhs = blk_v[r, x].reshape(len(ks) * blk_v.shape[-2], blk_v.shape[-1])
            part = jnp.dot(lhs, rhs, preferred_element_type=jnp.float32)
            if h == 0:
                acc[x] = part
            else:
                out_ref[x] = (acc[x] + part).astype(out_ref.dtype)


def ladder(places, head, tail, blocks):
    n_nar, n_x, per, t, s = blocks.shape
    n_k = n_nar * per
    rows = head.shape[1] + tail.shape[1]
    return pl.pallas_call(
        functools.partial(ladder_kernel, n_x, n_k, per),
        out_shape=jax.ShapeDtypeStruct((n_x, rows, s), jnp.bfloat16),
        in_specs=[
            pl.BlockSpec(memory_space=pltpu.SMEM),
            pl.BlockSpec(memory_space=pl.ANY),
            pl.BlockSpec(memory_space=pl.ANY),
            pl.BlockSpec(memory_space=pl.ANY),
        ],
        out_specs=pl.BlockSpec(memory_space=pltpu.VMEM),
        scratch_shapes=[
            pltpu.VMEM(head.shape, head.dtype),
            pltpu.VMEM(tail.shape, tail.dtype),
            pltpu.VMEM(blocks.shape, blocks.dtype),
            pltpu.VMEM((n_x, rows, s), jnp.float32),
            pltpu.SemaphoreType.DMA((4,)),
        ],
        cost_estimate=pl.CostEstimate(
            flops=2 * n_x * n_k * rows * t * s,
            transcendentals=0,
            bytes_accessed=2 * (2 * blocks.size + n_x * rows * s),
        ),
    )(places, head, tail, blocks)


def pick_kernel(n_out, cut, sel_ref, amp_ref, head_ref, tail_ref):
    def body(j, carry):
        tile = amp_ref[sel_ref[j]]
        head_ref[j] = tile[:cut]
        tail_ref[j] = tile[cut:]
        return carry

    lax.fori_loop(0, n_out, body, 0)


def pick_outgoing(amplitudes, selection, cut):
    n_out, (rows, t) = selection.shape[0], amplitudes.shape[1:]
    return pl.pallas_call(
        functools.partial(pick_kernel, n_out, cut),
        out_shape=(
            jax.ShapeDtypeStruct((n_out, cut, t), amplitudes.dtype),
            jax.ShapeDtypeStruct((n_out, rows - cut, t), amplitudes.dtype),
        ),
        in_specs=[pl.BlockSpec(memory_space=pltpu.SMEM), pl.BlockSpec(memory_space=pltpu.VMEM)],
        out_specs=(pl.BlockSpec(memory_space=pltpu.VMEM), pl.BlockSpec(memory_space=pltpu.VMEM)),
        cost_estimate=pl.CostEstimate(flops=0, transcendentals=0, bytes_accessed=4 * n_out * amplitudes[0].size),
    )(selection, amplitudes)


def on_device(n_nar, amplitudes, send_list, tile_positions, integrals):
    head, tail = pick_outgoing(amplitudes, send_list[0], CUT)
    head = lax.all_to_all(head, "wide", split_axis=0, concat_axis=0, tiled=True)
    tail = lax.all_to_all(tail, "wide", split_axis=0, concat_axis=0, tiled=True)
    lanes = jnp.zeros((tile_positions.shape[0], 128), tile_positions.dtype)
    lanes = lax.dynamic_update_slice(lanes, tile_positions, (0, 0))
    blocks, places = gather_integrals(integrals, lanes, n_nar)
    return ladder(places, head, tail, blocks)


def solution(mesh):
    placed = (
        P("wide", "narrow", None),
        P("wide", None),
        P("wide", "narrow"),
        P("wide", "narrow", None, None),
    )
    return jax.shard_map(
        functools.partial(on_device, mesh.shape["narrow"]),
        mesh=mesh,
        in_specs=placed,
        out_specs=P("wide", "narrow", None),
        check_vma=False,
    )
```

```python
import functools

import jax
import jax.numpy as jnp
from jax import lax
from jax.experimental import pallas as pl
from jax.experimental.pallas import tpu as pltpu
from jax.sharding import PartitionSpec as P

MESH = pl.DeviceIdType.MESH
CUT = 48


def gather_kernel(n_nar, src_ref, pos_ref, dst_ref, pos_dst, send_sem, recv_sem, local_sem):
    me = lax.axis_index("narrow")
    w = lax.axis_index("wide")

    barrier = pltpu.get_barrier_semaphore()
    for i in range(1, n_nar):
        peer = lax.rem(me + i, n_nar)
        pl.semaphore_signal(barrier, 1, device_id=(w, peer), device_id_type=MESH)
    pl.semaphore_wait(barrier, n_nar - 1)

    locals_ = [
        pltpu.make_async_copy(src_ref, dst_ref.at[me], local_sem.at[0]),
        pltpu.make_async_copy(pos_ref, pos_dst.at[me], local_sem.at[1]),
    ]
    for c in locals_:
        c.start()

    def remote(peer, slot):
        return [
            pltpu.make_async_remote_copy(
                src_ref=s,
                dst_ref=d.at[slot],
                send_sem=send_sem.at[part, peer],
                recv_sem=recv_sem.at[part, slot],
                device_id=(w, peer),
                device_id_type=MESH,
            )
            for part, (s, d) in enumerate(((src_ref, dst_ref), (pos_ref, pos_dst)))
        ]

    for i in range(1, n_nar):
        for c in remote(lax.rem(me + i, n_nar), me):
            c.start()
    for i in range(1, n_nar):
        for c in remote(lax.rem(me + i, n_nar), me):
            c.wait_send()
        owner = lax.rem(me + n_nar - i, n_nar)
        for c in remote(owner, owner):
            c.wait_recv()
    for c in locals_:
        c.wait()


def gather_integrals(integrals, positions, n_nar):
    return pl.pallas_call(
        functools.partial(gather_kernel, n_nar),
        out_shape=(
            jax.ShapeDtypeStruct((n_nar,) + integrals.shape, integrals.dtype),
            jax.ShapeDtypeStruct((n_nar,) + positions.shape, positions.dtype),
        ),
        in_specs=[pl.BlockSpec(memory_space=pl.ANY), pl.BlockSpec(memory_space=pl.ANY)],
        out_specs=(pl.BlockSpec(memory_space=pl.ANY), pl.BlockSpec(memory_space=pl.ANY)),
        scratch_shapes=[
            pltpu.SemaphoreType.DMA((2, n_nar)),
            pltpu.SemaphoreType.DMA((2, n_nar)),
            pltpu.SemaphoreType.DMA((2,)),
        ],
        compiler_params=pltpu.CompilerParams(collective_id=0, has_side_effects=True),
        cost_estimate=pl.CostEstimate(
            flops=0, transcendentals=0, bytes_accessed=2 * n_nar * integrals.size * 2
        ),
    )(integrals, positions)


def ladder_kernel(n_x, n_k, per, places_ref, head_hbm, tail_hbm, blk_hbm, out_ref, head_v, tail_v, blk_v, acc, sems):
    n_parts = 4
    step = blk_v.shape[0] // n_parts
    parts = [pl.ds(i * step, step) for i in range(n_parts)]
    copies = [
        pltpu.make_async_copy(head_hbm, head_v, sems.at[0]),
        pltpu.make_async_copy(tail_hbm, tail_v, sems.at[1]),
    ] + [pltpu.make_async_copy(blk_hbm.at[r], blk_v.at[r], sems.at[2 + i]) for i, r in enumerate(parts)]
    for c in copies:
        c.start()
    copies[0].wait()
    copies[1].wait()
    for h, r in enumerate(parts):
        copies[2 + h].wait()
        ks = range(h * step * per, (h + 1) * step * per)
        for x in range(n_x):
            picked = []
            for k in ks:
                p = places_ref[k // per, x, k % per]
                picked.append(jnp.concatenate([head_v[p], tail_v[p]], axis=0))
            lhs = jnp.concatenate(picked, axis=1)
            rhs = blk_v[r, x].reshape(len(ks) * blk_v.shape[-2], blk_v.shape[-1])
            part = jnp.dot(lhs, rhs, preferred_element_type=jnp.float32)
            if h == 0:
                acc[x] = part
            elif h < n_parts - 1:
                acc[x] = acc[x] + part
            else:
                out_ref[x] = (acc[x] + part).astype(out_ref.dtype)


def ladder(places, head, tail, blocks):
    n_nar, n_x, per, t, s = blocks.shape
    n_k = n_nar * per
    rows = head.shape[1] + tail.shape[1]
    return pl.pallas_call(
        functools.partial(ladder_kernel, n_x, n_k, per),
        out_shape=jax.ShapeDtypeStruct((n_x, rows, s), jnp.bfloat16),
        in_specs=[
            pl.BlockSpec(memory_space=pltpu.SMEM),
            pl.BlockSpec(memory_space=pl.ANY),
            pl.BlockSpec(memory_space=pl.ANY),
            pl.BlockSpec(memory_space=pl.ANY),
        ],
        out_specs=pl.BlockSpec(memory_space=pltpu.VMEM),
        scratch_shapes=[
            pltpu.VMEM(head.shape, head.dtype),
            pltpu.VMEM(tail.shape, tail.dtype),
            pltpu.VMEM(blocks.shape, blocks.dtype),
            pltpu.VMEM((n_x, rows, s), jnp.float32),
            pltpu.SemaphoreType.DMA((6,)),
        ],
        cost_estimate=pl.CostEstimate(
            flops=2 * n_x * n_k * rows * t * s,
            transcendentals=0,
            bytes_accessed=2 * (2 * blocks.size + n_x * rows * s),
        ),
    )(places, head, tail, blocks)


def pick_kernel(n_out, cut, sel_ref, amp_ref, head_ref, tail_ref):
    def body(j, carry):
        tile = amp_ref[sel_ref[j]]
        head_ref[j] = tile[:cut]
        tail_ref[j] = tile[cut:]
        return carry

    lax.fori_loop(0, n_out, body, 0)


def pick_outgoing(amplitudes, selection, cut):
    n_out, (rows, t) = selection.shape[0], amplitudes.shape[1:]
    return pl.pallas_call(
        functools.partial(pick_kernel, n_out, cut),
        out_shape=(
            jax.ShapeDtypeStruct((n_out, cut, t), amplitudes.dtype),
            jax.ShapeDtypeStruct((n_out, rows - cut, t), amplitudes.dtype),
        ),
        in_specs=[pl.BlockSpec(memory_space=pltpu.SMEM), pl.BlockSpec(memory_space=pltpu.VMEM)],
        out_specs=(pl.BlockSpec(memory_space=pltpu.VMEM), pl.BlockSpec(memory_space=pltpu.VMEM)),
        cost_estimate=pl.CostEstimate(flops=0, transcendentals=0, bytes_accessed=4 * n_out * amplitudes[0].size),
    )(selection, amplitudes)


def on_device(n_nar, amplitudes, send_list, tile_positions, integrals):
    head, tail = pick_outgoing(amplitudes, send_list[0], CUT)
    head = lax.all_to_all(head, "wide", split_axis=0, concat_axis=0, tiled=True)
    tail = lax.all_to_all(tail, "wide", split_axis=0, concat_axis=0, tiled=True)
    lanes = jnp.zeros((tile_positions.shape[0], 128), tile_positions.dtype)
    lanes = lax.dynamic_update_slice(lanes, tile_positions, (0, 0))
    blocks, places = gather_integrals(integrals, lanes, n_nar)
    return ladder(places, head, tail, blocks)


def solution(mesh):
    placed = (
        P("wide", "narrow", None),
        P("wide", None),
        P("wide", "narrow"),
        P("wide", "narrow", None, None),
    )
    return jax.shard_map(
        functools.partial(on_device, mesh.shape["narrow"]),
        mesh=mesh,
        in_specs=placed,
        out_specs=P("wide", "narrow", None),
        check_vma=False,
    )
```

```python
import functools

import jax
import jax.numpy as jnp
from jax import lax
from jax.experimental import pallas as pl
from jax.experimental.pallas import tpu as pltpu
from jax.sharding import PartitionSpec as P

MESH = pl.DeviceIdType.MESH
CUT = 64


def gather_kernel(n_nar, src_ref, pos_ref, dst_ref, pos_dst, send_sem, recv_sem, local_sem):
    me = lax.axis_index("narrow")
    w = lax.axis_index("wide")

    barrier = pltpu.get_barrier_semaphore()
    for i in range(1, n_nar):
        peer = lax.rem(me + i, n_nar)
        pl.semaphore_signal(barrier, 1, device_id=(w, peer), device_id_type=MESH)
    pl.semaphore_wait(barrier, n_nar - 1)

    locals_ = [
        pltpu.make_async_copy(src_ref, dst_ref.at[me], local_sem.at[0]),
        pltpu.make_async_copy(pos_ref, pos_dst.at[me], local_sem.at[1]),
    ]
    for c in locals_:
        c.start()

    def remote(peer, slot):
        return [
            pltpu.make_async_remote_copy(
                src_ref=s,
                dst_ref=d.at[slot],
                send_sem=send_sem.at[part, peer],
                recv_sem=recv_sem.at[part, slot],
                device_id=(w, peer),
                device_id_type=MESH,
            )
            for part, (s, d) in enumerate(((src_ref, dst_ref), (pos_ref, pos_dst)))
        ]

    for i in range(1, n_nar):
        for c in remote(lax.rem(me + i, n_nar), me):
            c.start()
    for i in range(1, n_nar):
        for c in remote(lax.rem(me + i, n_nar), me):
            c.wait_send()
        owner = lax.rem(me + n_nar - i, n_nar)
        for c in remote(owner, owner):
            c.wait_recv()
    for c in locals_:
        c.wait()


def gather_integrals(integrals, positions, n_nar):
    return pl.pallas_call(
        functools.partial(gather_kernel, n_nar),
        out_shape=(
            jax.ShapeDtypeStruct((n_nar,) + integrals.shape, integrals.dtype),
            jax.ShapeDtypeStruct((n_nar,) + positions.shape, positions.dtype),
        ),
        in_specs=[pl.BlockSpec(memory_space=pl.ANY), pl.BlockSpec(memory_space=pl.ANY)],
        out_specs=(pl.BlockSpec(memory_space=pl.ANY), pl.BlockSpec(memory_space=pl.ANY)),
        scratch_shapes=[
            pltpu.SemaphoreType.DMA((2, n_nar)),
            pltpu.SemaphoreType.DMA((2, n_nar)),
            pltpu.SemaphoreType.DMA((2,)),
        ],
        compiler_params=pltpu.CompilerParams(collective_id=0, has_side_effects=True),
        cost_estimate=pl.CostEstimate(
            flops=0, transcendentals=0, bytes_accessed=2 * n_nar * integrals.size * 2
        ),
    )(integrals, positions)


def ladder_kernel(n_x, n_k, per, places_ref, head_hbm, tail_hbm, blk_hbm, out_ref, head_v, tail_v, blk_v, acc, sems):
    half = blk_v.shape[0] // 2
    parts = (pl.ds(0, half), pl.ds(half, blk_v.shape[0] - half))
    copies = [
        pltpu.make_async_copy(head_hbm, head_v, sems.at[0]),
        pltpu.make_async_copy(tail_hbm, tail_v, sems.at[1]),
    ] + [pltpu.make_async_copy(blk_hbm.at[r], blk_v.at[r], sems.at[2 + i]) for i, r in enumerate(parts)]
    for c in copies:
        c.start()
    for c in copies[:3]:
        c.wait()
    for h, r in enumerate(parts):
        if h == 1:
            copies[3].wait()
        ks = range(h * half * per, (h * half + r.size) * per)
        for x in range(n_x):
            picked = []
            for k in ks:
                p = places_ref[k // per, x, k % per]
                picked.append(jnp.concatenate([head_v[p], tail_v[p]], axis=0))
            lhs = jnp.concatenate(picked, axis=1)
            rhs = blk_v[r, x].reshape(len(ks) * blk_v.shape[-2], blk_v.shape[-1])
            part = jnp.dot(lhs, rhs, preferred_element_type=jnp.float32)
            if h == 0:
                acc[x] = part
            else:
                out_ref[x] = (acc[x] + part).astype(out_ref.dtype)


def ladder(places, head, tail, blocks):
    n_nar, n_x, per, t, s = blocks.shape
    n_k = n_nar * per
    rows = head.shape[1] + tail.shape[1]
    return pl.pallas_call(
        functools.partial(ladder_kernel, n_x, n_k, per),
        out_shape=jax.ShapeDtypeStruct((n_x, rows, s), jnp.bfloat16),
        in_specs=[
            pl.BlockSpec(memory_space=pltpu.SMEM),
            pl.BlockSpec(memory_space=pl.ANY),
            pl.BlockSpec(memory_space=pl.ANY),
            pl.BlockSpec(memory_space=pl.ANY),
        ],
        out_specs=pl.BlockSpec(memory_space=pltpu.VMEM),
        scratch_shapes=[
            pltpu.VMEM(head.shape, head.dtype),
            pltpu.VMEM(tail.shape, tail.dtype),
            pltpu.VMEM(blocks.shape, blocks.dtype),
            pltpu.VMEM((n_x, rows, s), jnp.float32),
            pltpu.SemaphoreType.DMA((4,)),
        ],
        cost_estimate=pl.CostEstimate(
            flops=2 * n_x * n_k * rows * t * s,
            transcendentals=0,
            bytes_accessed=2 * (2 * blocks.size + n_x * rows * s),
        ),
    )(places, head, tail, blocks)


def pick_kernel(n_out, cut, sel_ref, amp_ref, head_ref, tail_ref):
    def body(j, carry):
        tile = amp_ref[sel_ref[j]]
        head_ref[j] = tile[:cut]
        tail_ref[j] = tile[cut:]
        return carry

    lax.fori_loop(0, n_out, body, 0)


def pick_outgoing(amplitudes, selection, cut):
    n_out, (rows, t) = selection.shape[0], amplitudes.shape[1:]
    return pl.pallas_call(
        functools.partial(pick_kernel, n_out, cut),
        out_shape=(
            jax.ShapeDtypeStruct((n_out, cut, t), amplitudes.dtype),
            jax.ShapeDtypeStruct((n_out, rows - cut, t), amplitudes.dtype),
        ),
        in_specs=[pl.BlockSpec(memory_space=pltpu.SMEM), pl.BlockSpec(memory_space=pltpu.VMEM)],
        out_specs=(pl.BlockSpec(memory_space=pltpu.VMEM), pl.BlockSpec(memory_space=pltpu.VMEM)),
        cost_estimate=pl.CostEstimate(flops=0, transcendentals=0, bytes_accessed=4 * n_out * amplitudes[0].size),
    )(selection, amplitudes)


def on_device(n_nar, amplitudes, send_list, tile_positions, integrals):
    head, tail = pick_outgoing(amplitudes, send_list[0], CUT)
    head = lax.all_to_all(head, "wide", split_axis=0, concat_axis=0, tiled=True)
    tail = lax.all_to_all(tail, "wide", split_axis=0, concat_axis=0, tiled=True)
    lanes = jnp.zeros((tile_positions.shape[0], 128), tile_positions.dtype)
    lanes = lax.dynamic_update_slice(lanes, tile_positions, (0, 0))
    blocks, places = gather_integrals(integrals, lanes, n_nar)
    return ladder(places, head, tail, blocks)


def solution(mesh):
    placed = (
        P("wide", "narrow", None),
        P("wide", None),
        P("wide", "narrow"),
        P("wide", "narrow", None, None),
    )
    return jax.shard_map(
        functools.partial(on_device, mesh.shape["narrow"]),
        mesh=mesh,
        in_specs=placed,
        out_specs=P("wide", "narrow", None),
        check_vma=False,
    )
```

```python
import functools

import jax
import jax.numpy as jnp
from jax import lax
from jax.experimental import pallas as pl
from jax.experimental.pallas import tpu as pltpu
from jax.sharding import PartitionSpec as P

MESH = pl.DeviceIdType.MESH
CUT = 48


def gather_kernel(n_nar, src_ref, pos_ref, dst_ref, pos_dst, send_sem, recv_sem, local_sem):
    me = lax.axis_index("narrow")
    w = lax.axis_index("wide")

    barrier = pltpu.get_barrier_semaphore()
    for i in range(1, n_nar):
        peer = lax.rem(me + i, n_nar)
        pl.semaphore_signal(barrier, 1, device_id=(w, peer), device_id_type=MESH)
    pl.semaphore_wait(barrier, n_nar - 1)

    locals_ = [
        pltpu.make_async_copy(src_ref, dst_ref.at[me], local_sem.at[0]),
        pltpu.make_async_copy(pos_ref, pos_dst.at[me], local_sem.at[1]),
    ]
    for c in locals_:
        c.start()

    def remote(peer, slot):
        return [
            pltpu.make_async_remote_copy(
                src_ref=s,
                dst_ref=d.at[slot],
                send_sem=send_sem.at[part, peer],
                recv_sem=recv_sem.at[part, slot],
                device_id=(w, peer),
                device_id_type=MESH,
            )
            for part, (s, d) in enumerate(((src_ref, dst_ref), (pos_ref, pos_dst)))
        ]

    for i in range(1, n_nar):
        for c in remote(lax.rem(me + i, n_nar), me):
            c.start()
    for i in range(1, n_nar):
        for c in remote(lax.rem(me + i, n_nar), me):
            c.wait_send()
        owner = lax.rem(me + n_nar - i, n_nar)
        for c in remote(owner, owner):
            c.wait_recv()
    for c in locals_:
        c.wait()


def gather_integrals(integrals, positions, n_nar):
    return pl.pallas_call(
        functools.partial(gather_kernel, n_nar),
        out_shape=(
            jax.ShapeDtypeStruct((n_nar,) + integrals.shape, integrals.dtype),
            jax.ShapeDtypeStruct((n_nar,) + positions.shape, positions.dtype),
        ),
        in_specs=[pl.BlockSpec(memory_space=pl.ANY), pl.BlockSpec(memory_space=pl.ANY)],
        out_specs=(pl.BlockSpec(memory_space=pl.ANY), pl.BlockSpec(memory_space=pl.ANY)),
        scratch_shapes=[
            pltpu.SemaphoreType.DMA((2, n_nar)),
            pltpu.SemaphoreType.DMA((2, n_nar)),
            pltpu.SemaphoreType.DMA((2,)),
        ],
        compiler_params=pltpu.CompilerParams(collective_id=0, has_side_effects=True),
        cost_estimate=pl.CostEstimate(
            flops=0, transcendentals=0, bytes_accessed=2 * n_nar * integrals.size * 2
        ),
    )(integrals, positions)


def ladder_kernel(n_x, n_k, per, places_ref, head_hbm, tail_hbm, blk_hbm, out_ref, head_v, tail_v, blk_v, acc, sems):
    half = blk_v.shape[0] // 2
    parts = (pl.ds(0, half), pl.ds(half, blk_v.shape[0] - half))
    copies = [
        pltpu.make_async_copy(head_hbm, head_v, sems.at[0]),
        pltpu.make_async_copy(tail_hbm, tail_v, sems.at[1]),
    ] + [pltpu.make_async_copy(blk_hbm.at[r], blk_v.at[r], sems.at[2 + i]) for i, r in enumerate(parts)]
    for c in copies:
        c.start()
    for c in copies[:3]:
        c.wait()
    for h, r in enumerate(parts):
        if h == 1:
            copies[3].wait()
        ks = range(h * half * per, (h * half + r.size) * per)
        for x in range(n_x):
            picked = []
            for k in ks:
                p = places_ref[k // per, x, k % per]
                picked.append(jnp.concatenate([head_v[p], tail_v[p]], axis=0))
            lhs = jnp.concatenate(picked, axis=1)
            rhs = blk_v[r, x].reshape(len(ks) * blk_v.shape[-2], blk_v.shape[-1])
            part = jnp.dot(lhs, rhs, preferred_element_type=jnp.float32)
            if h == 0:
                acc[x] = part
            else:
                out_ref[x] = (acc[x] + part).astype(out_ref.dtype)


def ladder(places, head, tail, blocks):
    n_nar, n_x, per, t, s = blocks.shape
    n_k = n_nar * per
    rows = head.shape[1] + tail.shape[1]
    return pl.pallas_call(
        functools.partial(ladder_kernel, n_x, n_k, per),
        out_shape=jax.ShapeDtypeStruct((n_x, rows, s), jnp.bfloat16),
        in_specs=[
            pl.BlockSpec(memory_space=pltpu.SMEM),
            pl.BlockSpec(memory_space=pl.ANY),
            pl.BlockSpec(memory_space=pl.ANY),
            pl.BlockSpec(memory_space=pl.ANY),
        ],
        out_specs=pl.BlockSpec(memory_space=pltpu.VMEM),
        scratch_shapes=[
            pltpu.VMEM(head.shape, head.dtype),
            pltpu.VMEM(tail.shape, tail.dtype),
            pltpu.VMEM(blocks.shape, blocks.dtype),
            pltpu.VMEM((n_x, rows, s), jnp.float32),
            pltpu.SemaphoreType.DMA((4,)),
        ],
        cost_estimate=pl.CostEstimate(
            flops=2 * n_x * n_k * rows * t * s,
            transcendentals=0,
            bytes_accessed=2 * (2 * blocks.size + n_x * rows * s),
        ),
    )(places, head, tail, blocks)


def pick_kernel(n_out, cut, n_chunks, sel_ref, amp_ref, head_hbm, tail_hbm, head_v, tail_v, sems):
    size = n_out // n_chunks

    def body(j, carry):
        tile = amp_ref[sel_ref[j]]
        head_v[j] = tile[:cut]
        tail_v[j] = tile[cut:]
        return carry

    copies = []
    for c in range(n_chunks):
        lax.fori_loop(c * size, (c + 1) * size, body, 0)
        r = pl.ds(c * size, size)
        for i, (v, h) in enumerate(((head_v, head_hbm), (tail_v, tail_hbm))):
            copies.append(pltpu.make_async_copy(v.at[r], h.at[r], sems.at[i, c]))
            copies[-1].start()
    for cp in copies:
        cp.wait()


def pick_outgoing(amplitudes, selection, cut):
    n_out, (rows, t) = selection.shape[0], amplitudes.shape[1:]
    n_chunks = 4
    return pl.pallas_call(
        functools.partial(pick_kernel, n_out, cut, n_chunks),
        out_shape=(
            jax.ShapeDtypeStruct((n_out, cut, t), amplitudes.dtype),
            jax.ShapeDtypeStruct((n_out, rows - cut, t), amplitudes.dtype),
        ),
        in_specs=[pl.BlockSpec(memory_space=pltpu.SMEM), pl.BlockSpec(memory_space=pltpu.VMEM)],
        out_specs=(pl.BlockSpec(memory_space=pl.ANY), pl.BlockSpec(memory_space=pl.ANY)),
        scratch_shapes=[
            pltpu.VMEM((n_out, cut, t), amplitudes.dtype),
            pltpu.VMEM((n_out, rows - cut, t), amplitudes.dtype),
            pltpu.SemaphoreType.DMA((2, n_chunks)),
        ],
        cost_estimate=pl.CostEstimate(flops=0, transcendentals=0, bytes_accessed=4 * n_out * amplitudes[0].size),
    )(selection, amplitudes)


def on_device(n_nar, amplitudes, send_list, tile_positions, integrals):
    head, tail = pick_outgoing(amplitudes, send_list[0], CUT)
    head = lax.all_to_all(head, "wide", split_axis=0, concat_axis=0, tiled=True)
    tail = lax.all_to_all(tail, "wide", split_axis=0, concat_axis=0, tiled=True)
    lanes = jnp.zeros((tile_positions.shape[0], 128), tile_positions.dtype)
    lanes = lax.dynamic_update_slice(lanes, tile_positions, (0, 0))
    blocks, places = gather_integrals(integrals, lanes, n_nar)
    return ladder(places, head, tail, blocks)


def solution(mesh):
    placed = (
        P("wide", "narrow", None),
        P("wide", None),
        P("wide", "narrow"),
        P("wide", "narrow", None, None),
    )
    return jax.shard_map(
        functools.partial(on_device, mesh.shape["narrow"]),
        mesh=mesh,
        in_specs=placed,
        out_specs=P("wide", "narrow", None),
        check_vma=False,
    )
```

```python
import functools

import jax
import jax.numpy as jnp
from jax import lax
from jax.experimental import pallas as pl
from jax.experimental.pallas import tpu as pltpu
from jax.sharding import PartitionSpec as P

MESH = pl.DeviceIdType.MESH
CUT = 48


def gather_kernel(n_nar, src_ref, pos_ref, dst_ref, pos_dst, send_sem, recv_sem, local_sem):
    me = lax.axis_index("narrow")
    w = lax.axis_index("wide")

    barrier = pltpu.get_barrier_semaphore()
    for i in range(1, n_nar):
        peer = lax.rem(me + i, n_nar)
        pl.semaphore_signal(barrier, 1, device_id=(w, peer), device_id_type=MESH)
    pl.semaphore_wait(barrier, n_nar - 1)

    locals_ = [
        pltpu.make_async_copy(src_ref, dst_ref.at[me], local_sem.at[0]),
        pltpu.make_async_copy(pos_ref, pos_dst.at[me], local_sem.at[1]),
    ]
    for c in locals_:
        c.start()

    def remote(peer, slot):
        return [
            pltpu.make_async_remote_copy(
                src_ref=s,
                dst_ref=d.at[slot],
                send_sem=send_sem.at[part, peer],
                recv_sem=recv_sem.at[part, slot],
                device_id=(w, peer),
                device_id_type=MESH,
            )
            for part, (s, d) in enumerate(((src_ref, dst_ref), (pos_ref, pos_dst)))
        ]

    for i in range(1, n_nar):
        for c in remote(lax.rem(me + i, n_nar), me):
            c.start()
    for i in range(1, n_nar):
        for c in remote(lax.rem(me + i, n_nar), me):
            c.wait_send()
        owner = lax.rem(me + n_nar - i, n_nar)
        for c in remote(owner, owner):
            c.wait_recv()
    for c in locals_:
        c.wait()


def gather_integrals(integrals, positions, n_nar):
    return pl.pallas_call(
        functools.partial(gather_kernel, n_nar),
        out_shape=(
            jax.ShapeDtypeStruct((n_nar,) + integrals.shape, integrals.dtype),
            jax.ShapeDtypeStruct((n_nar,) + positions.shape, positions.dtype),
        ),
        in_specs=[pl.BlockSpec(memory_space=pl.ANY), pl.BlockSpec(memory_space=pl.ANY)],
        out_specs=(pl.BlockSpec(memory_space=pl.ANY), pl.BlockSpec(memory_space=pl.ANY)),
        scratch_shapes=[
            pltpu.SemaphoreType.DMA((2, n_nar)),
            pltpu.SemaphoreType.DMA((2, n_nar)),
            pltpu.SemaphoreType.DMA((2,)),
        ],
        compiler_params=pltpu.CompilerParams(collective_id=0, has_side_effects=True),
        cost_estimate=pl.CostEstimate(
            flops=0, transcendentals=0, bytes_accessed=2 * n_nar * integrals.size * 2
        ),
    )(integrals, positions)


def ladder_kernel(n_x, n_k, per, places_ref, head_hbm, tail_hbm, blk_hbm, out_ref, head_v, tail_v, blk_v, acc, sems):
    half = blk_v.shape[0] // 2
    parts = (pl.ds(0, half), pl.ds(half, blk_v.shape[0] - half))
    copies = [
        pltpu.make_async_copy(head_hbm, head_v, sems.at[0]),
        pltpu.make_async_copy(tail_hbm, tail_v, sems.at[1]),
    ] + [pltpu.make_async_copy(blk_hbm.at[r], blk_v.at[r], sems.at[2 + i]) for i, r in enumerate(parts)]
    for c in copies:
        c.start()
    for c in copies[:3]:
        c.wait()
    for h, r in enumerate(parts):
        if h == 1:
            copies[3].wait()
        ks = range(h * half * per, (h * half + r.size) * per)
        for x in range(n_x):
            picked = []
            for k in ks:
                p = places_ref[k // per, x, k % per]
                picked.append(jnp.concatenate([head_v[p], tail_v[p]], axis=0))
            lhs = jnp.concatenate(picked, axis=1)
            rhs = blk_v[r, x].reshape(len(ks) * blk_v.shape[-2], blk_v.shape[-1])
            part = jnp.dot(lhs, rhs, preferred_element_type=jnp.float32)
            if h == 0:
                acc[x] = part
            else:
                out_ref[x] = (acc[x] + part).astype(out_ref.dtype)


def ladder(places, head, tail, blocks):
    n_nar, n_x, per, t, s = blocks.shape
    n_k = n_nar * per
    rows = head.shape[1] + tail.shape[1]
    return pl.pallas_call(
        functools.partial(ladder_kernel, n_x, n_k, per),
        out_shape=jax.ShapeDtypeStruct((n_x, rows, s), jnp.bfloat16),
        in_specs=[
            pl.BlockSpec(memory_space=pltpu.SMEM),
            pl.BlockSpec(memory_space=pl.ANY),
            pl.BlockSpec(memory_space=pl.ANY),
            pl.BlockSpec(memory_space=pl.ANY),
        ],
        out_specs=pl.BlockSpec(memory_space=pltpu.VMEM),
        scratch_shapes=[
            pltpu.VMEM(head.shape, head.dtype),
            pltpu.VMEM(tail.shape, tail.dtype),
            pltpu.VMEM(blocks.shape, blocks.dtype),
            pltpu.VMEM((n_x, rows, s), jnp.float32),
            pltpu.SemaphoreType.DMA((4,)),
        ],
        cost_estimate=pl.CostEstimate(
            flops=2 * n_x * n_k * rows * t * s,
            transcendentals=0,
            bytes_accessed=2 * (2 * blocks.size + n_x * rows * s),
        ),
    )(places, head, tail, blocks)


def pick_kernel(n_out, cut, n_chunks, sel_ref, amp_ref, head_hbm, tail_hbm, head_v, tail_v, sems):
    size = n_out // n_chunks

    def body(j, carry):
        tile = amp_ref[sel_ref[j]]
        head_v[j] = tile[:cut]
        tail_v[j] = tile[cut:]
        return carry

    copies = []
    for c in range(n_chunks):
        lax.fori_loop(c * size, (c + 1) * size, body, 0)
        r = pl.ds(c * size, size)
        for i, (v, h) in enumerate(((head_v, head_hbm), (tail_v, tail_hbm))):
            copies.append(pltpu.make_async_copy(v.at[r], h.at[r], sems.at[i, c]))
            copies[-1].start()
    for cp in copies:
        cp.wait()


def pick_outgoing(amplitudes, selection, cut):
    n_out, (rows, t) = selection.shape[0], amplitudes.shape[1:]
    n_chunks = 8
    return pl.pallas_call(
        functools.partial(pick_kernel, n_out, cut, n_chunks),
        out_shape=(
            jax.ShapeDtypeStruct((n_out, cut, t), amplitudes.dtype),
            jax.ShapeDtypeStruct((n_out, rows - cut, t), amplitudes.dtype),
        ),
        in_specs=[pl.BlockSpec(memory_space=pltpu.SMEM), pl.BlockSpec(memory_space=pltpu.VMEM)],
        out_specs=(pl.BlockSpec(memory_space=pl.ANY), pl.BlockSpec(memory_space=pl.ANY)),
        scratch_shapes=[
            pltpu.VMEM((n_out, cut, t), amplitudes.dtype),
            pltpu.VMEM((n_out, rows - cut, t), amplitudes.dtype),
            pltpu.SemaphoreType.DMA((2, n_chunks)),
        ],
        cost_estimate=pl.CostEstimate(flops=0, transcendentals=0, bytes_accessed=4 * n_out * amplitudes[0].size),
    )(selection, amplitudes)


def on_device(n_nar, amplitudes, send_list, tile_positions, integrals):
    head, tail = pick_outgoing(amplitudes, send_list[0], CUT)
    head = lax.all_to_all(head, "wide", split_axis=0, concat_axis=0, tiled=True)
    tail = lax.all_to_all(tail, "wide", split_axis=0, concat_axis=0, tiled=True)
    lanes = jnp.zeros((tile_positions.shape[0], 128), tile_positions.dtype)
    lanes = lax.dynamic_update_slice(lanes, tile_positions, (0, 0))
    blocks, places = gather_integrals(integrals, lanes, n_nar)
    return ladder(places, head, tail, blocks)


def solution(mesh):
    placed = (
        P("wide", "narrow", None),
        P("wide", None),
        P("wide", "narrow"),
        P("wide", "narrow", None, None),
    )
    return jax.shard_map(
        functools.partial(on_device, mesh.shape["narrow"]),
        mesh=mesh,
        in_specs=placed,
        out_specs=P("wide", "narrow", None),
        check_vma=False,
    )
```
